128 devices in a mesh: row: 4 (over y), col: 32 (over z, x, core).
Axes of the slice: x: 4, y: 4, z: 4, core: 2. Of those that a mesh axis runs over, the one named last changes fastest.
Arguments:
- lower_panel: float32 [32, 6, 5, 2, 256, 256], P('col', None, None, None, 'row'), may hold values from -0.0625 to 0.0625
- diag_inverse: float32 [32, 6, 2, 256, 256], P('col', None, None, 'row'), may hold values from -3 to 3, as said below
- structure: int32 [32, 6, 5], P('col'), may hold values 0 or 1
Outputs:
- sel_panel: float32 [32, 6, 5, 2, 256, 256], P('col', None, None, None, 'row')
- sel_diag: float32 [32, 6, 2, 256, 256], P('col', None, None, 'row')
The draws below stay inside these ranges and needn't reach their ends.
Inputs may be any that keep to these rules, and one draw needn't show every extreme that they name: Every block diag_inverse[c, s, k] equals its own transpose.
All inputs are finite; a program needn't handle non-finite values. No bound on the sum of `structure` on one device may be relied on, other than what follows from the above.
Results may differ from the reference program's by a relative error of at most 0.0001.
Values sent between devices are 32-bit elements; how exact they have to be, the bound alone decides.
A program may use at most 128 MiB of HBM per device.

```python
import math
import jax
import jax.numpy as jnp
from jax import lax

W = 256
LEVELS = 6
ANC = 5
SLOTS = 6
N_COL = 32


def draw_diag_inverse(key, part):
    shape = (N_COL, SLOTS, 2, W, W)
    first_key, second_key = jax.random.split(key)
    noise_draw = jax.random.normal(first_key, shape, jnp.float32)
    symmetric = (noise_draw + jnp.swapaxes(noise_draw, -1, -2)) * (0.5 / math.sqrt(W))
    row_ids = lax.broadcasted_iota(jnp.int32, (W, W), 0)
    col_ids = lax.broadcasted_iota(jnp.int32, (W, W), 1)
    identity = (row_ids == col_ids).astype(jnp.float32)
    scales = jax.random.uniform(second_key, (N_COL, SLOTS, 2, W), jnp.float32, 0.5, 1.5)
    real_only = (lax.broadcasted_iota(jnp.int32, (2, 1, 1), 0) == 0).astype(jnp.float32)
    return symmetric + identity * scales[..., None] * real_only


def plant(values, key, smallest, top_value):
    longest = values.shape.index(max(values.shape))
    spots = []
    for shift in (0, 1):
        where = [jax.random.randint(jax.random.fold_in(key, axis), (), 0, length) for axis, length in enumerate(values.shape)]
        where[longest] = (where[longest] + shift) % values.shape[longest]
        spots.append(tuple(where))
    return values.at[spots[0]].set(smallest).at[spots[1]].set(top_value)


def block_scale(stream_key, shape, cuts, least, high):
    loudness, own = 1.0, jax.random.fold_in(stream_key, 6)
    for axis_at, blocks in cuts:
        draws = jnp.exp(jax.random.uniform(jax.random.fold_in(own, axis_at), (blocks,), jnp.float32, least / len(cuts), high / len(cuts)))
        loudness = loudness * jnp.repeat(draws, shape[axis_at] // blocks).reshape([-1 if axis == axis_at else 1 for axis in range(len(shape))])
    return loudness


def noise(stream_key, extent, width, reach, shards=(), dtype=jnp.bfloat16):
    array = jax.random.normal(stream_key, extent, jnp.float32) * width
    if len(shards) > 0:
        array = block_scale(stream_key, extent, shards, -0.22, 0.18) * array
    return jnp.clip(array, min=-reach, max=reach).astype(dtype)


def setup_inputs(seed: int = 0) -> dict:
    key_list = jax.random.split(jax.random.key(seed), 4)
    return {
        "lower_panel": noise(key_list[0], (N_COL, SLOTS, ANC, 2, W, W), (8 * ANC * W) ** -0.5, 0.0625, ((0, 32), (4, 4)), jnp.float32),
        "diag_inverse": draw_diag_inverse(jax.random.fold_in(key_list[3], 71), 0),
        "structure": plant((jax.random.randint(key_list[2], (N_COL, SLOTS, ANC), 0, 4) < 3).astype(jnp.int32), jax.random.fold_in(key_list[2], 1), 0, 1),
    }


def complex_product(first_factor, second_factor):
    highest = lax.Precision.HIGHEST
    real_part = jnp.dot(first_factor[0], second_factor[0], precision=highest) - jnp.dot(first_factor[1], second_factor[1], precision=highest)
    imag_part = jnp.dot(first_factor[0], second_factor[1], precision=highest) + jnp.dot(first_factor[1], second_factor[0], precision=highest)
    return jnp.stack([real_part, imag_part])


def transposed(matrix):
    return jnp.swapaxes(matrix, -1, -2)


def reference(lower_panel, diag_inverse, structure):
    block_width = lower_panel.shape[-1]
    slot_count = lower_panel.shape[1]
    anc_count = lower_panel.shape[2]
    zero_panel = jnp.zeros((anc_count, 2, block_width, block_width), jnp.float32)
    zero_block = jnp.zeros((2, block_width, block_width), jnp.float32)
    panel_table = [[zero_panel for slot_index in range(slot_count)] for column in range(N_COL)]
    diag_table = [[zero_block for slot_index in range(slot_count)] for column in range(N_COL)]
    previous = {}
    offset = 0
    for tree_depth in range(LEVELS):
        per_col = max(1, 2 ** tree_depth // N_COL)
        current = {}
        for member in range(2 ** tree_depth):
            column = (member * N_COL) // 2 ** tree_depth
            slot_index = offset + member % per_col
            inverse_block = diag_inverse[column, slot_index]
            if tree_depth == 0:
                diagonal = inverse_block
                chain_new = inverse_block
            else:
                present = structure[column, slot_index, :tree_depth].astype(jnp.float32)
                panels = lower_panel[column, slot_index, :tree_depth] * present[:, None, None, None]
                stacked = jnp.concatenate([panels[row_pos] for row_pos in range(tree_depth)], axis=1)
                parent_chain = previous[member // 2]
                lifted = -complex_product(parent_chain, stacked)
                diagonal = inverse_block - complex_product(transposed(stacked), lifted)
                top_row = jnp.concatenate([diagonal, transposed(lifted)], axis=2)
                bottom_rows = jnp.concatenate([lifted, parent_chain], axis=2)
                chain_new = jnp.concatenate([top_row, bottom_rows], axis=1)
                pieces = [lifted[:, row_pos * block_width:(row_pos + 1) * block_width] for row_pos in range(tree_depth)]
                pieces = pieces + [zero_block for row_pos in range(anc_count - tree_depth)]
                panel_table[column][slot_index] = jnp.stack(pieces)
            diag_table[column][slot_index] = diagonal
            current[member] = chain_new
        previous = current
        offset = offset + per_col
    sel_panel = jnp.stack([jnp.stack(panel_table[column]) for column in range(N_COL)])
    sel_diag = jnp.stack([jnp.stack(diag_table[column]) for column in range(N_COL)])
    return sel_panel, sel_diag
```

```python
import functools

import jax
import jax.numpy as jnp
from jax import lax
from jax.experimental import pallas as pl
from jax.experimental.pallas import tpu as pltpu
from jax.sharding import PartitionSpec as P

LEVELS = 6
MESH = pl.DeviceIdType.MESH
F32 = jnp.float32
BF16 = jnp.bfloat16
W = 256

X_AT = (None, 1, 3)
D_AT = (0, 2, 5)


def split(x):
    high = x.astype(BF16)
    return high, (x - high.astype(F32)).astype(BF16)


def mm(a, b):
    return jnp.dot(a, b, preferred_element_type=F32)


def kernel(
    lp, dg, panel, diag,
    f012, f3, f4, f5, gh, gl, xh, xl, rb1, rb2, rb3, rb4, lh, ll, pk, yo, zo, zb, dl,
    p1r, s0, s1, s2, s3, s4, ys, yr, xs, xr, cs, cr, os, ls,
):
    row = lax.axis_index("row")
    col = lax.axis_index("col")
    core = lax.rem(col, 2)
    xpos = lax.rem(col // 2, 4)
    plane = (col // 8) * 8
    up, down = lax.rem(row + 1, 4), lax.rem(row + 3, 4)
    xup, xdown = lax.rem(xpos + 1, 4), lax.rem(xpos + 3, 4)
    xfar = lax.rem(xpos + 2, 4)
    to_row = lambda r: {"row": r, "col": col}
    to_x = lambda x: {"row": row, "col": plane + 2 * x + core}
    other = {"row": row, "col": col + 1 - 2 * core}
    rbs = (None, rb1, rb2, rb3, rb4)
    my_rows = pl.ds(pl.multiple_of(row * 64, 64), 64)

    def remote(src, dst, send, recv, device):
        return pltpu.make_async_remote_copy(
            src_ref=src, dst_ref=dst, send_sem=send, recv_sem=recv, device_id=device, device_id_type=MESH
        )

    def pieces(d, j):
        kk = lax.rem(j, 2)
        if d <= 2:
            xx = lax.rem(j // 2, 4)
            part = pl.ds(pl.multiple_of(lax.rem(j, 8) * 8, 8), 8)
            out = [(dg.at[d, :, part], f012.at[D_AT[d], :, row, xx, kk])]
            if d:
                out.append((lp.at[d, 0:d, :, part], f012.at[X_AT[d] : X_AT[d] + d, :, row, xx, kk]))
            return out
        part = pl.ds(pl.multiple_of(kk * 32, 32), 32)
        buf = f3 if d == 3 else f4
        return [
            (dg.at[d, :, part], buf.at[d, :, row, kk]),
            (lp.at[d, 0:d, :, part], buf.at[0:d, :, row, kk]),
        ]

    sends = (s0, s1, s2, s3, s4)

    def home_copy(d, i, j):
        src, dst = pieces(d, j)[i]
        return remote(src, dst, sends[d].at[j - 1, i], p1r.at[d, i], {"row": row, "col": col + j})

    def is_home(d):
        return lax.rem(col, 2 ** (5 - d)) == 0

    def n_pieces(d):
        return 2 if d else 1

    def home_start(d):
        @pl.when(is_home(d))
        def _():
            for i, (src, dst) in enumerate(pieces(d, 0)):
                pltpu.make_async_copy(src, dst, p1r.at[d, i]).start()

            def step(j, carry):
                for i in range(n_pieces(d)):
                    home_copy(d, i, j).start()
                return carry

            lax.fori_loop(1, 2 ** (5 - d), step, 0)

    def home_finish(d):
        @pl.when(is_home(d))
        def _():
            def step(j, carry):
                for i in range(n_pieces(d)):
                    home_copy(d, i, j).wait_send()
                return carry

            lax.fori_loop(1, 2 ** (5 - d), step, 0)

    def piece_wait(d):
        for i, (_, dst) in enumerate(pieces(d, lax.rem(col, 8))):
            pltpu.make_async_copy(dst, dst, p1r.at[d, i]).wait()

    def y_slice(n, r, half=None):
        h = slice(None) if half is None else half
        if n == 0:
            return f012.at[:, h, r, xpos, core]
        if n == 1:
            return f3.at[:, h, r, core]
        if n == 2:
            return f4.at[:, h, r, core]
        return f5.at[n - 3, h, r]

    def y_copy(n, q):
        src = lp.at[5, n - 3] if n >= 3 else y_slice(n, row)
        if q == 0:
            args = (src, y_slice(n, row), up)
        elif q == 1:
            args = (src, y_slice(n, row), down)
        elif q == 2:
            args = (y_slice(n, down, 0), y_slice(n, down, 0), up)
        else:
            args = (y_slice(n, up, 1), y_slice(n, up, 1), down)
        return remote(args[0], args[1], ys.at[n, q], yr.at[n, q], to_row(args[2]))

    def y_first(n):
        y_copy(n, 0).start()
        y_copy(n, 1).start()

    def y_forward(n):
        y_copy(n, 0).wait_recv()
        y_copy(n, 2).start()
        y_copy(n, 1).wait_recv()
        y_copy(n, 3).start()

    def y_done(n):
        y_copy(n, 2).wait_recv()
        y_copy(n, 3).wait_recv()

    def x_copy(q):
        own = f012.at[:, :, :, xpos, core]
        if q == 0:
            args = (own, xup)
        elif q == 1:
            args = (own, xdown)
        elif q == 2:
            args = (f012.at[:, 0, :, xdown, core], xup)
        else:
            args = (f012.at[:, 1, :, xup, core], xdown)
        return remote(args[0], args[0], xs.at[q], xr.at[q], to_x(args[1]))

    def core_copy(q):
        if q < 4:
            ref = f012.at[:, :, :, (xpos, xdown, xup, xfar)[q], core]
        elif q == 4:
            ref = f3.at[:, :, :, core]
        else:
            ref = f4.at[:, :, :, core]
        return remote(ref, ref, cs.at[q], cr.at[q], other)

    leaf_own = pltpu.make_async_copy(lp.at[5], f5.at[:, :, row], ls.at[0])
    leaf_own.start()
    d_leaf = pltpu.make_async_copy(dg.at[5], dl.at[0], ls.at[1])
    d_leaf.start()
    d_root = pltpu.make_async_copy(dg.at[0], dl.at[1], ls.at[2])
    d_root.start()

    for d in range(5):
        home_start(d)
    y_first(3)
    y_first(4)
    for d in range(3):
        piece_wait(d)
    y_first(0)
    piece_wait(3)
    y_first(1)
    piece_wait(4)
    y_first(2)
    for n in range(5, 8):
        y_first(n)

    zb[...] = jnp.zeros_like(zb)
    zeros = [pltpu.make_async_copy(zb.at[0 : 5 - d], panel.at[d, d:5], os.at[0, d]) for d in range(5)]
    for copy in zeros:
        copy.start()

    y_forward(0)
    y_done(0)
    x_copy(0).start()
    x_copy(1).start()
    core_copy(0).start()
    y_forward(1)
    x_copy(0).wait_recv()
    x_copy(2).start()
    core_copy(1).start()
    x_copy(1).wait_recv()
    x_copy(3).start()
    core_copy(2).start()
    y_forward(2)
    y_done(1)
    core_copy(4).start()
    x_copy(2).wait_recv()
    x_copy(3).wait_recv()
    core_copy(3).start()
    y_forward(3)
    y_forward(4)

    d_root.wait()
    root_out = pltpu.make_async_copy(dl.at[1], diag.at[0], os.at[2, 0])
    root_out.start()
    for q in range(4):
        core_copy(q).wait_recv()

    def block(d, a, part):
        if d <= 2:
            return f012[X_AT[d] + a, part].reshape(W, W)
        if d == 3:
            return f3[a, part].reshape(W, W)
        if d == 4:
            return f4[a, part].reshape(W, W)
        return f5[a, part].reshape(W, W)

    def d_block(d, part):
        if d <= 2:
            return f012[D_AT[d], part].reshape(W, W)
        return (f3 if d == 3 else f4)[d, part].reshape(W, W)

    def put(high, low, rows, cols, real, imag):
        for m, value in enumerate((real, imag, real + imag)):
            h, l = split(value)
            high[m, rows, cols] = h
            low[m, rows, cols] = l

    def prepare(d):
        def step(f, carry):
            rows = pl.ds(pl.multiple_of(f * W, W), W)
            a = d - 1 - f
            put(xh, xl, rows, slice(None), block(d, a, 0), block(d, a, 1))
            return carry

        lax.fori_loop(0, d, step, 0)

    def three(high, low, rows, depth):
        out = []
        for m in range(3):
            a_high = high[m, rows, 0:depth]
            b_high = xh[m, 0:depth, :]
            acc = mm(a_high, b_high) + mm(a_high, xl[m, 0:depth, :])
            out.append(acc + mm(low[m, rows, 0:depth], b_high))
        return out[1] - out[0], out[0] + out[1] - out[2]

    put(gh, gl, slice(0, W), slice(0, W), d_block(0, 0), d_block(0, 1))

    outs = []

    def level(d):
        prepare(d)
        rb = rbs[d]
        depth = d * W
        new = slice(depth, depth + W)

        def step(e, carry):
            at = pl.ds(pl.multiple_of(e * W, W), W)
            real, imag = three(gh, gl, at, depth)
            last = (e == d).astype(F32)
            real = real + last * d_block(d, 0)
            imag = imag + last * d_block(d, 1)
            slot = jnp.where(e == d, d, d - 1 - e)
            rb[slot, 0] = real
            rb[slot, 1] = imag
            put(gh, gl, at, new, real, imag)
            put(gh, gl, new, at, real.T, imag.T)
            return carry

        lax.fori_loop(0, d + 1, step, 0)
        copies = [
            pltpu.make_async_copy(rb.at[0:d, :, my_rows], panel.at[d, 0:d], os.at[1, d]),
            pltpu.make_async_copy(rb.at[d, :, my_rows], diag.at[d], os.at[2, d]),
        ]
        for copy in copies:
            copy.start()
        outs.extend(copies)

    level(1)
    level(2)
    y_done(2)
    core_copy(5).start()
    core_copy(4).wait_recv()
    level(3)
    y_forward(5)
    y_forward(6)
    core_copy(5).wait_recv()
    level(4)
    y_forward(7)
    leaf_own.wait()
    for n in range(3, 8):
        y_done(n)

    prepare(5)

    def pick(x):
        out = x[:, 0:64]
        for r in range(1, 4):
            out = jnp.where(row == r, x[:, 64 * r : 64 * r + 64], out)
        return out

    def pack(f, carry):
        rows = pl.ds(pl.multiple_of(f * W, W), W)
        real, imag = pick(block(5, 4 - f, 0)), pick(block(5, 4 - f, 1))
        rh, rl = split(real)
        ih, il = split(imag)
        pk[rows, :] = jnp.concatenate([v.astype(F32) for v in (rh, ih, rl, il)], axis=1).astype(BF16)
        return carry

    lax.fori_loop(0, 5, pack, 0)

    def columns(e, carry):
        at = pl.ds(pl.multiple_of(e * W, W), W)
        p = pk[...]
        a = mm(gh[0, at, :], p) + mm(gl[0, at, :], p)
        b = mm(gh[1, at, :], p) + mm(gl[1, at, :], p)
        real = b[:, 64:128] + b[:, 192:256] - a[:, 0:64] - a[:, 128:192]
        imag = -(a[:, 64:128] + a[:, 192:256] + b[:, 0:64] + b[:, 128:192])
        flipped = jnp.concatenate([real, imag], axis=1).T
        put(lh, ll, slice(320, 384), at, flipped[0:64], flipped[64:128])
        mine = pl.ds(pl.multiple_of(e * W + row * 64, 64), 64)
        to = pl.ds(pl.multiple_of(e * 64, 64), 64)
        for m in range(3):
            lh[m, to, :] = gh[m, mine, :]
            ll[m, to, :] = gl[m, mine, :]
        return carry

    lax.fori_loop(0, 5, columns, 0)
    real, imag = three(lh, ll, slice(0, 384), 5 * W)
    for e in range(5):
        yo[4 - e, 0] = real[64 * e : 64 * e + 64]
        yo[4 - e, 1] = imag[64 * e : 64 * e + 64]
    d_leaf.wait()
    zo[0] = dl[0, 0] + real[320:384]
    zo[1] = dl[0, 1] + imag[320:384]
    copies = [
        pltpu.make_async_copy(yo, panel.at[5], os.at[1, 5]),
        pltpu.make_async_copy(zo, diag.at[5], os.at[2, 5]),
    ]
    for copy in copies:
        copy.start()

    for d in range(5):
        home_finish(d)
    for n in range(8):
        for q in range(4):
            y_copy(n, q).wait_send()
    for q in range(4):
        x_copy(q).wait_send()
    for q in range(6):
        core_copy(q).wait_send()
    for copy in zeros + [root_out] + outs + copies:
        copy.wait()


def inverse_blocks(lp, dg):
    dma = pltpu.SemaphoreType.DMA
    vmem = pltpu.VMEM
    side = 5 * W
    any_spec = pl.BlockSpec(memory_space=pl.ANY)
    return pl.pallas_call(
        kernel,
        out_shape=(
            jax.ShapeDtypeStruct((6, 5, 2, 64, W), F32),
            jax.ShapeDtypeStruct((6, 2, 64, W), F32),
        ),
        in_specs=[any_spec] * 2,
        out_specs=(any_spec, any_spec),
        scratch_shapes=[
            vmem((6, 2, 4, 4, 2, 8, W), F32),
            vmem((4, 2, 4, 2, 32, W), F32),
            vmem((5, 2, 4, 2, 32, W), F32),
            vmem((5, 2, 4, 64, W), F32),
            vmem((3, side, side), BF16),
            vmem((3, side, side), BF16),
            vmem((3, side, W), BF16),
            vmem((3, side, W), BF16),
            vmem((2, 2, W, W), F32),
            vmem((3, 2, W, W), F32),
            vmem((4, 2, W, W), F32),
            vmem((5, 2, W, W), F32),
            vmem((3, 384, side), BF16),
            vmem((3, 384, side), BF16),
            vmem((side, W), BF16),
            vmem((5, 2, 64, W), F32),
            vmem((2, 64, W), F32),
            vmem((5, 2, 64, W), F32),
            vmem((2, 2, 64, W), F32),
            dma((5, 2)),
            dma((31, 1)),
            dma((15, 2)),
            dma((7, 2)),
            dma((3, 2)),
            dma((1, 2)),
            dma((8, 4)),
            dma((8, 4)),
            dma((4,)),
            dma((4,)),
            dma((6,)),
            dma((6,)),
            dma((3, 6)),
            dma((3,)),
        ],
        compiler_params=pltpu.CompilerParams(vmem_limit_bytes=66_000_000, has_side_effects=True),
        name="inverse_blocks",
    )(lp, dg)


def body(lower_panel, diag_inverse, structure):
    masked = lower_panel[0] * structure[0].astype(F32)[:, :, None, None, None]
    panel, diag = inverse_blocks(masked, diag_inverse[0])
    position = lax.axis_index("col")
    strides = 2 ** (5 - jnp.arange(LEVELS))
    active = position % strides == 0
    panel = jnp.where(active[:, None, None, None, None], panel, 0.0)
    diag = jnp.where(active[:, None, None, None], diag, 0.0)
    return panel[None], diag[None]


def solution(mesh):
    in_specs = (
        P("col", None, None, None, "row", None),
        P("col", None, None, "row", None),
        P("col", None, None),
    )
    out_specs = (P("col", None, None, None, "row", None), P("col", None, None, "row", None))
    return jax.shard_map(body, mesh=mesh, in_specs=in_specs, out_specs=out_specs, check_vma=False)
```

```python
import functools

import jax
import jax.numpy as jnp
from jax import lax
from jax.experimental import pallas as pl
from jax.experimental.pallas import tpu as pltpu
from jax.sharding import PartitionSpec as P

LEVELS = 6
MESH = pl.DeviceIdType.MESH
F32 = jnp.float32
BF16 = jnp.bfloat16
W = 256

AT = (None, 0, 1, 3, 6)
OUT = (0, 1, 3, 6, 10, 15)
X_AT = (None, 1, 3)
D_AT = (0, 2, 5)


def split(x):
    high = x.astype(BF16)
    return high, (x - high.astype(F32)).astype(BF16)


def mm(a, b):
    return jnp.dot(a, b, preferred_element_type=F32)


def kernel(
    st, lp, dg, out,
    f012, f3, f4, f5, lv, gh, gl, xh1, xl1, xh3, xl3, xh4, xl4, xh, xl, rb1, rb2, rb3, rb4, lh, ll, pk, yo, zo, dl,
    p1r, s0, s1, s2, s3, s4, ys, yr, xs, xr, cs, cr, os, ls,
):
    row = lax.axis_index("row")
    col = lax.axis_index("col")
    core = lax.rem(col, 2)
    xpos = lax.rem(col // 2, 4)
    plane = (col // 8) * 8
    up, down = lax.rem(row + 1, 4), lax.rem(row + 3, 4)
    xup, xdown = lax.rem(xpos + 1, 4), lax.rem(xpos + 3, 4)
    xfar = lax.rem(xpos + 2, 4)
    to_row = lambda r: {"row": r, "col": col}
    to_x = lambda x: {"row": row, "col": plane + 2 * x + core}
    other = {"row": row, "col": col + 1 - 2 * core}
    rbs = (None, rb1, rb2, rb3, rb4)
    my_rows = pl.ds(pl.multiple_of(row * 64, 64), 64)

    def is_home(d):
        return lax.rem(col, 2 ** (5 - d)) == 0

    def tell(device):
        pl.semaphore_signal(pltpu.get_barrier_semaphore(), inc=1, device_id=device, device_id_type=MESH)

    for device in (other, to_row(up), to_row(down), to_x(xup), to_x(xdown)):
        tell(device)
    for d in range(5):
        @pl.when(jnp.logical_not(is_home(d)))
        def _():
            size = 2 ** (5 - d)
            tell({"row": row, "col": (col // size) * size})

    loads = [pltpu.make_async_copy(lp.at[5], f5.at[:, :, row], ls.at[5])]
    for d in range(1, 5):
        loads.append(pltpu.make_async_copy(lp.at[d, 0:d], lv.at[AT[d] : AT[d] + d], ls.at[d]))
    d_leaf = pltpu.make_async_copy(dg.at[5], dl.at[0], ls.at[0])
    d_root = pltpu.make_async_copy(dg.at[0], dl.at[1], ls.at[6])
    for copy in loads + [d_leaf, d_root]:
        copy.start()
    loads[0].wait()
    for a in range(5):
        f5[a, :, row] = f5[a, :, row] * st[25 + a].astype(F32)
    for d in range(1, 5):
        loads[d].wait()
        for a in range(d):
            lv[AT[d] + a] = lv[AT[d] + a] * st[5 * d + a].astype(F32)

    callers = 5
    for d in range(5):
        callers = callers + is_home(d).astype(jnp.int32) * (2 ** (5 - d) - 1)
    pl.semaphore_wait(pltpu.get_barrier_semaphore(), callers)

    def remote(src, dst, send, recv, device):
        return pltpu.make_async_remote_copy(
            src_ref=src, dst_ref=dst, send_sem=send, recv_sem=recv, device_id=device, device_id_type=MESH
        )

    def pieces(d, j):
        kk = lax.rem(j, 2)
        mine = lv.at[AT[d] : AT[d] + d] if d else None
        if d <= 2:
            xx = lax.rem(j // 2, 4)
            part = pl.ds(pl.multiple_of(lax.rem(j, 8) * 8, 8), 8)
            out = [(dg.at[d, :, part], f012.at[D_AT[d], :, row, xx, kk])]
            if d:
                out.append((mine.at[:, :, part], f012.at[X_AT[d] : X_AT[d] + d, :, row, xx, kk]))
            return out
        part = pl.ds(pl.multiple_of(kk * 32, 32), 32)
        buf = f3 if d == 3 else f4
        return [
            (dg.at[d, :, part], buf.at[d, :, row, kk]),
            (mine.at[:, :, part], buf.at[0:d, :, row, kk]),
        ]

    sends = (s0, s1, s2, s3, s4)

    def home_copy(d, i, j):
        src, dst = pieces(d, j)[i]
        return remote(src, dst, sends[d].at[j - 1, i], p1r.at[d, i], {"row": row, "col": col + j})

    def n_pieces(d):
        return 2 if d else 1

    def home_start(d):
        @pl.when(is_home(d))
        def _():
            for i, (src, dst) in enumerate(pieces(d, 0)):
                pltpu.make_async_copy(src, dst, p1r.at[d, i]).start()

            def step(j, carry):
                for i in range(n_pieces(d)):
                    home_copy(d, i, j).start()
                return carry

            lax.fori_loop(1, 2 ** (5 - d), step, 0)

    def home_finish(d):
        @pl.when(is_home(d))
        def _():
            def step(j, carry):
                for i in range(n_pieces(d)):
                    home_copy(d, i, j).wait_send()
                return carry

            lax.fori_loop(1, 2 ** (5 - d), step, 0)

    def piece_wait(d):
        for i, (_, dst) in enumerate(pieces(d, lax.rem(col, 8))):
            pltpu.make_async_copy(dst, dst, p1r.at[d, i]).wait()

    def y_slice(n, r, half=None):
        h = slice(None) if half is None else half
        if n < 2:
            return f012.at[3 * n : 3 * n + 3, h, r, xpos, core]
        if n == 2:
            return f3.at[:, h, r, core]
        if n == 3:
            return f4.at[:, h, r, core]
        return f5.at[n - 4, h, r]

    def y_copy(n, q):
        if q == 0:
            ref, device = y_slice(n, row), up
        elif q == 1:
            ref, device = y_slice(n, row), down
        elif q == 2:
            ref, device = y_slice(n, down, 0), up
        else:
            ref, device = y_slice(n, up, 1), down
        return remote(ref, ref, ys.at[n, q], yr.at[n, q], to_row(device))

    def y_first(n):
        y_copy(n, 0).start()
        y_copy(n, 1).start()

    def y_forward(n):
        y_copy(n, 0).wait_recv()
        y_copy(n, 2).start()
        y_copy(n, 1).wait_recv()
        y_copy(n, 3).start()

    def y_done(n):
        y_copy(n, 2).wait_recv()
        y_copy(n, 3).wait_recv()

    def x_copy(c, q):
        blocks = f012.at[3 * c : 3 * c + 3]
        if q == 0:
            ref, device = blocks.at[:, :, :, xpos, core], xup
        elif q == 1:
            ref, device = blocks.at[:, :, :, xpos, core], xdown
        elif q == 2:
            ref, device = blocks.at[:, 0, :, xdown, core], xup
        else:
            ref, device = blocks.at[:, 1, :, xup, core], xdown
        return remote(ref, ref, xs.at[c, q], xr.at[c, q], to_x(device))

    def core_copy(q):
        if q < 8:
            ref = f012.at[3 * (q // 4) : 3 * (q // 4) + 3, :, :, (xpos, xdown, xup, xfar)[q % 4], core]
        elif q == 8:
            ref = f3.at[:, :, :, core]
        else:
            ref = f4.at[:, :, :, core]
        return remote(ref, ref, cs.at[q], cr.at[q], other)

    def x_first(c):
        y_done(c)
        x_copy(c, 0).start()
        x_copy(c, 1).start()
        core_copy(4 * c).start()

    def x_forward(c):
        x_copy(c, 0).wait_recv()
        x_copy(c, 2).start()
        core_copy(4 * c + 1).start()
        x_copy(c, 1).wait_recv()
        x_copy(c, 3).start()
        core_copy(4 * c + 2).start()

    def x_done(c):
        x_copy(c, 2).wait_recv()
        x_copy(c, 3).wait_recv()
        core_copy(4 * c + 3).start()

    def core_done(c):
        for q in range(4):
            core_copy(4 * c + q).wait_recv()

    for d in (0, 1, 2, 4, 3):
        home_start(d)
    y_first(4)
    piece_wait(0)
    piece_wait(1)
    y_first(0)
    piece_wait(2)
    y_first(1)
    y_first(5)
    y_forward(0)
    y_forward(1)
    piece_wait(4)
    y_first(3)
    x_first(0)
    x_first(1)
    piece_wait(3)
    y_first(2)
    y_forward(4)
    y_forward(5)
    y_first(6)
    x_forward(0)
    y_forward(3)
    x_done(0)
    x_forward(1)
    y_forward(2)
    y_first(7)
    y_first(8)
    d_root.wait()
    root_out = pltpu.make_async_copy(dl.at[1], out.at[0], os.at[0])
    root_out.start()

    def block(d, a, part):
        if d <= 2:
            return f012[X_AT[d] + a, part].reshape(W, W)
        if d == 3:
            return f3[a, part].reshape(W, W)
        if d == 4:
            return f4[a, part].reshape(W, W)
        return f5[a, part].reshape(W, W)

    def d_block(d, part):
        if d <= 2:
            return f012[D_AT[d], part].reshape(W, W)
        return (f3 if d == 3 else f4)[d, part].reshape(W, W)

    def put(high, low, rows, cols, real, imag):
        for m, value in enumerate((real, imag, real + imag)):
            h, l = split(value)
            high[m, rows, cols] = h
            low[m, rows, cols] = l

    xbufs = (None, (xh1, xl1), (xh1, xl1), (xh3, xl3), (xh4, xl4), (xh, xl))

    def prepare(d):
        high, low = xbufs[d]

        def step(f, carry):
            rows = pl.ds(pl.multiple_of(f * W, W), W)
            a = d - 1 - f
            put(high, low, rows, slice(None), block(d, a, 0), block(d, a, 1))
            return carry

        lax.fori_loop(0, d, step, 0)

    def three(high, low, rows, depth):
        x_high, x_low = xbufs[depth // W]
        out = []
        for m in range(3):
            a_high = high[m, rows, 0:depth]
            b_high = x_high[m, 0:depth, :]
            acc = mm(a_high, b_high) + mm(a_high, x_low[m, 0:depth, :])
            out.append(acc + mm(low[m, rows, 0:depth], b_high))
        return out[1] - out[0], out[0] + out[1] - out[2]


    outs = []

    def level(d):
        rb = rbs[d]
        depth = d * W
        new = slice(depth, depth + W)

        def step(e, carry):
            at = pl.ds(pl.multiple_of(e * W, W), W)
            real, imag = three(gh, gl, at, depth)
            last = (e == d).astype(F32)
            real = real + last * d_block(d, 0)
            imag = imag + last * d_block(d, 1)
            slot = jnp.where(e == d, d, d - 1 - e)
            rb[slot, 0] = real
            rb[slot, 1] = imag
            put(gh, gl, at, new, real, imag)
            put(gh, gl, new, at, real.T, imag.T)
            return carry

        lax.fori_loop(0, d + 1, step, 0)
        copies = [
            pltpu.make_async_copy(rb.at[:, :, my_rows], out.at[OUT[d] : OUT[d] + d + 1], os.at[d]),
        ]
        for copy in copies:
            copy.start()
        outs.extend(copies)

    y_done(2)
    core_copy(8).start()
    core_done(0)
    put(gh, gl, slice(0, W), slice(0, W), d_block(0, 0), d_block(0, 1))
    prepare(1)
    level(1)
    x_done(1)
    y_done(3)
    core_copy(9).start()
    y_forward(6)
    core_copy(8).wait_recv()
    prepare(3)
    core_done(1)
    prepare(2)
    level(2)
    y_forward(7)
    core_copy(9).wait_recv()
    level(3)
    y_forward(8)
    prepare(4)
    level(4)
    for n in range(4, 9):
        y_done(n)

    prepare(5)

    def pick(x):
        out = x[:, 0:64]
        for r in range(1, 4):
            out = jnp.where(row == r, x[:, 64 * r : 64 * r + 64], out)
        return out

    def pack(f, carry):
        rows = pl.ds(pl.multiple_of(f * W, W), W)
        real, imag = pick(block(5, 4 - f, 0)), pick(block(5, 4 - f, 1))
        rh, rl = split(real)
        ih, il = split(imag)
        pk[rows, :] = jnp.concatenate([v.astype(F32) for v in (rh, ih, rl, il)], axis=1).astype(BF16)
        return carry

    lax.fori_loop(0, 5, pack, 0)

    def columns(e, carry):
        at = pl.ds(pl.multiple_of(e * W, W), W)
        p = pk[...]
        a = mm(gh[0, at, :], p) + mm(gl[0, at, :], p)
        b = mm(gh[1, at, :], p) + mm(gl[1, at, :], p)
        real = b[:, 64:128] + b[:, 192:256] - a[:, 0:64] - a[:, 128:192]
        imag = -(a[:, 64:128] + a[:, 192:256] + b[:, 0:64] + b[:, 128:192])
        flipped = jnp.concatenate([real, imag], axis=1).T
        put(lh, ll, slice(320, 384), at, flipped[0:64], flipped[64:128])
        mine = pl.ds(pl.multiple_of(e * W + row * 64, 64), 64)
        to = pl.ds(pl.multiple_of(e * 64, 64), 64)
        for m in range(3):
            lh[m, to, :] = gh[m, mine, :]
            ll[m, to, :] = gl[m, mine, :]
        return carry

    lax.fori_loop(0, 5, columns, 0)
    real, imag = three(lh, ll, slice(0, 384), 5 * W)
    for e in range(5):
        yo[4 - e, 0] = real[64 * e : 64 * e + 64]
        yo[4 - e, 1] = imag[64 * e : 64 * e + 64]
    d_leaf.wait()
    zo[0] = dl[0, 0] + real[320:384]
    zo[1] = dl[0, 1] + imag[320:384]
    copies = [
        pltpu.make_async_copy(yo, out.at[15:20], os.at[5]),
        pltpu.make_async_copy(zo, out.at[20], os.at[6]),
    ]
    for copy in copies:
        copy.start()

    for d in range(5):
        home_finish(d)
    for n in range(9):
        for q in range(4):
            y_copy(n, q).wait_send()
    for c in range(2):
        for q in range(4):
            x_copy(c, q).wait_send()
    for q in range(10):
        core_copy(q).wait_send()
    for copy in [root_out] + outs + copies:
        copy.wait()


def inverse_blocks(st, lp, dg):
    dma = pltpu.SemaphoreType.DMA
    vmem = pltpu.VMEM
    side = 5 * W
    any_spec = pl.BlockSpec(memory_space=pl.ANY)
    return pl.pallas_call(
        kernel,
        out_shape=jax.ShapeDtypeStruct((21, 2, 64, W), F32),
        in_specs=[pl.BlockSpec(memory_space=pltpu.SMEM), any_spec, any_spec],
        out_specs=any_spec,
        scratch_shapes=[
            vmem((6, 2, 4, 4, 2, 8, W), F32),
            vmem((4, 2, 4, 2, 32, W), F32),
            vmem((5, 2, 4, 2, 32, W), F32),
            vmem((5, 2, 4, 64, W), F32),
            vmem((10, 2, 64, W), F32),
            vmem((3, side, side), BF16),
            vmem((3, side, side), BF16),
            vmem((3, 2 * W, W), BF16),
            vmem((3, 2 * W, W), BF16),
            vmem((3, 3 * W, W), BF16),
            vmem((3, 3 * W, W), BF16),
            vmem((3, 4 * W, W), BF16),
            vmem((3, 4 * W, W), BF16),
            vmem((3, side, W), BF16),
            vmem((3, side, W), BF16),
            vmem((2, 2, W, W), F32),
            vmem((3, 2, W, W), F32),
            vmem((4, 2, W, W), F32),
            vmem((5, 2, W, W), F32),
            vmem((3, 384, side), BF16),
            vmem((3, 384, side), BF16),
            vmem((side, W), BF16),
            vmem((5, 2, 64, W), F32),
            vmem((2, 64, W), F32),
            vmem((2, 2, 64, W), F32),
            dma((5, 2)),
            dma((31, 1)),
            dma((15, 2)),
            dma((7, 2)),
            dma((3, 2)),
            dma((1, 2)),
            dma((9, 4)),
            dma((9, 4)),
            dma((2, 4)),
            dma((2, 4)),
            dma((10,)),
            dma((10,)),
            dma((7,)),
            dma((7,)),
        ],
        compiler_params=pltpu.CompilerParams(
            vmem_limit_bytes=66_000_000, has_side_effects=True, collective_id=1
        ),
        name="inverse_blocks",
    )(st, lp, dg)


def spread(src, panel, diag, buf, zero, rs, ws):
    col = lax.axis_index("col")

    def active(d):
        return lax.rem(col, 2 ** (5 - d)) == 0

    def read(d):
        at = slice(OUT[d], OUT[d] + d + 1)
        return pltpu.make_async_copy(src.at[at], buf.at[at], rs.at[d])

    for d in range(LEVELS):
        @pl.when(active(d))
        def _():
            read(d).start()

    zero[...] = jnp.zeros_like(zero)
    for d in range(5):
        pltpu.make_async_copy(zero.at[0 : 5 - d], panel.at[d, d:5], ws.at[0, d]).start()

    def write(d, real):
        blocks = buf if real else zero
        at = OUT[d] if real else 0
        out = [pltpu.make_async_copy(blocks.at[at + d if real else 0], diag.at[d], ws.at[1, d])]
        if d:
            out.append(pltpu.make_async_copy(blocks.at[at : at + d], panel.at[d, 0:d], ws.at[2, d]))
        return out

    for d in range(5):
        @pl.when(jnp.logical_not(active(d)))
        def _():
            for copy in write(d, False):
                copy.start()

    for d in range(LEVELS):
        @pl.when(active(d))
        def _():
            read(d).wait()
            for copy in write(d, True):
                copy.start()

    for d in range(5):
        pltpu.make_async_copy(zero.at[0 : 5 - d], panel.at[d, d:5], ws.at[0, d]).wait()
    for d in range(LEVELS):
        for copy in write(d, True):
            copy.wait()


def spread_out(blocks):
    dma = pltpu.SemaphoreType.DMA
    any_spec = pl.BlockSpec(memory_space=pl.ANY)
    return pl.pallas_call(
        spread,
        out_shape=(
            jax.ShapeDtypeStruct((6, 5, 2, 64, W), F32),
            jax.ShapeDtypeStruct((6, 2, 64, W), F32),
        ),
        in_specs=[any_spec],
        out_specs=(any_spec, any_spec),
        scratch_shapes=[
            pltpu.VMEM((21, 2, 64, W), F32),
            pltpu.VMEM((5, 2, 64, W), F32),
            dma((6,)),
            dma((3, 6)),
        ],
        name="spread_out",
    )(blocks)


def body(lower_panel, diag_inverse, structure):
    blocks = inverse_blocks(structure.reshape(30), lower_panel[0], diag_inverse[0])
    panel, diag = spread_out(blocks)
    return panel[None], diag[None]


def solution(mesh):
    in_specs = (
        P("col", None, None, None, "row", None),
        P("col", None, None, "row", None),
        P("col", None, None),
    )
    out_specs = (P("col", None, None, None, "row", None), P("col", None, None, "row", None))
    return jax.shard_map(body, mesh=mesh, in_specs=in_specs, out_specs=out_specs, check_vma=False)
```

```python
import functools

import jax
import jax.numpy as jnp
from jax import lax
from jax.experimental import pallas as pl
from jax.experimental.pallas import tpu as pltpu
from jax.sharding import PartitionSpec as P

LEVELS = 6
MESH = pl.DeviceIdType.MESH
F32 = jnp.float32
BF16 = jnp.bfloat16
W = 256

AT = (None, 0, 1, 3, 6)
OUT = (0, 1, 3, 6, 10, 15)
X_AT = (None, 1, 3)
D_AT = (0, 2, 5)


def split(x):
    high = x.astype(BF16)
    return high, (x - high.astype(F32)).astype(BF16)


def mm(a, b):
    return jnp.dot(a, b, preferred_element_type=F32)


def kernel(
    st, lp, dg, out,
    f012, f3, f4, f5, lv, xnh, xnl, xth, xtl, dnh, dnl, u, uh, ul, v, vh, vl, lh, ll, yo, no, dl,
    p1r, s0, s1, s2, s3, s4, ys, yr, xs, xr, cs, cr, os, ls, ns, nr,
):
    row = lax.axis_index("row")
    col = lax.axis_index("col")
    core = lax.rem(col, 2)
    xpos = lax.rem(col // 2, 4)
    plane = (col // 8) * 8
    up, down = lax.rem(row + 1, 4), lax.rem(row + 3, 4)
    xup, xdown = lax.rem(xpos + 1, 4), lax.rem(xpos + 3, 4)
    xfar = lax.rem(xpos + 2, 4)
    to_row = lambda r: {"row": r, "col": col}
    to_x = lambda x: {"row": row, "col": plane + 2 * x + core}
    other = {"row": row, "col": col + 1 - 2 * core}
    my_rows = pl.ds(pl.multiple_of(row * 64, 64), 64)

    def is_home(d):
        return lax.rem(col, 2 ** (5 - d)) == 0

    def tell(device):
        pl.semaphore_signal(pltpu.get_barrier_semaphore(), inc=1, device_id=device, device_id_type=MESH)

    for device in (other, to_row(up), to_row(down), to_x(xup), to_x(xdown)):
        tell(device)
    for d in range(5):
        @pl.when(jnp.logical_not(is_home(d)))
        def _():
            size = 2 ** (5 - d)
            tell({"row": row, "col": (col // size) * size})

    loads = [pltpu.make_async_copy(lp.at[5], f5.at[:, :, row], ls.at[5])]
    for d in range(1, 5):
        loads.append(pltpu.make_async_copy(lp.at[d, 0:d], lv.at[AT[d] : AT[d] + d], ls.at[d]))
    d_leaf = pltpu.make_async_copy(dg.at[5], dl.at[0], ls.at[0])
    d_root = pltpu.make_async_copy(dg.at[0], dl.at[1], ls.at[6])
    for copy in loads + [d_leaf, d_root]:
        copy.start()
    loads[0].wait()
    for a in range(5):
        f5[a, :, row] = f5[a, :, row] * st[0, 5, a].astype(F32)
    for d in range(1, 5):
        loads[d].wait()
        for a in range(d):
            lv[AT[d] + a] = lv[AT[d] + a] * st[0, d, a].astype(F32)

    callers = 5
    for d in range(5):
        callers = callers + is_home(d).astype(jnp.int32) * (2 ** (5 - d) - 1)
    pl.semaphore_wait(pltpu.get_barrier_semaphore(), callers)

    def remote(src, dst, send, recv, device):
        return pltpu.make_async_remote_copy(
            src_ref=src, dst_ref=dst, send_sem=send, recv_sem=recv, device_id=device, device_id_type=MESH
        )

    def pieces(d, j):
        kk = lax.rem(j, 2)
        mine = lv.at[AT[d] : AT[d] + d] if d else None
        if d <= 2:
            xx = lax.rem(j // 2, 4)
            part = pl.ds(pl.multiple_of(lax.rem(j, 8) * 8, 8), 8)
            out = [(dg.at[d, :, part], f012.at[D_AT[d], :, row, xx, kk])]
            if d:
                out.append((mine.at[:, :, part], f012.at[X_AT[d] : X_AT[d] + d, :, row, xx, kk]))
            return out
        part = pl.ds(pl.multiple_of(kk * 32, 32), 32)
        buf = f3 if d == 3 else f4
        return [
            (dg.at[d, :, part], buf.at[d, :, row, kk]),
            (mine.at[:, :, part], buf.at[0:d, :, row, kk]),
        ]

    sends = (s0, s1, s2, s3, s4)

    def home_copy(d, i, j):
        src, dst = pieces(d, j)[i]
        return remote(src, dst, sends[d].at[j - 1, i], p1r.at[d, i], {"row": row, "col": col + j})

    def n_pieces(d):
        return 2 if d else 1

    def home_start(d):
        @pl.when(is_home(d))
        def _():
            for i, (src, dst) in enumerate(pieces(d, 0)):
                pltpu.make_async_copy(src, dst, p1r.at[d, i]).start()

            def step(j, carry):
                for i in range(n_pieces(d)):
                    home_copy(d, i, j).start()
                return carry

            lax.fori_loop(1, 2 ** (5 - d), step, 0)

    def home_finish(d):
        @pl.when(is_home(d))
        def _():
            def step(j, carry):
                for i in range(n_pieces(d)):
                    home_copy(d, i, j).wait_send()
                return carry

            lax.fori_loop(1, 2 ** (5 - d), step, 0)

    def piece_wait(d):
        for i, (_, dst) in enumerate(pieces(d, lax.rem(col, 8))):
            pltpu.make_async_copy(dst, dst, p1r.at[d, i]).wait()

    def y_slice(n, r, half=None):
        h = slice(None) if half is None else half
        if n < 2:
            return f012.at[3 * n : 3 * n + 3, h, r, xpos, core]
        if n == 2:
            return f3.at[:, h, r, core]
        if n == 3:
            return f4.at[:, h, r, core]
        return f5.at[n - 4, h, r]

    def y_copy(n, q):
        if q == 0:
            ref, device = y_slice(n, row), up
        elif q == 1:
            ref, device = y_slice(n, row), down
        elif q == 2:
            ref, device = y_slice(n, down, 0), up
        else:
            ref, device = y_slice(n, up, 1), down
        return remote(ref, ref, ys.at[n, q], yr.at[n, q], to_row(device))

    def y_first(n):
        y_copy(n, 0).start()
        y_copy(n, 1).start()

    def y_forward(n):
        y_copy(n, 0).wait_recv()
        y_copy(n, 2).start()
        y_copy(n, 1).wait_recv()
        y_copy(n, 3).start()

    def y_done(n):
        y_copy(n, 2).wait_recv()
        y_copy(n, 3).wait_recv()

    def x_copy(c, q):
        blocks = f012.at[3 * c : 3 * c + 3]
        if q == 0:
            ref, device = blocks.at[:, :, :, xpos, core], xup
        elif q == 1:
            ref, device = blocks.at[:, :, :, xpos, core], xdown
        elif q == 2:
            ref, device = blocks.at[:, 0, :, xdown, core], xup
        else:
            ref, device = blocks.at[:, 1, :, xup, core], xdown
        return remote(ref, ref, xs.at[c, q], xr.at[c, q], to_x(device))

    def core_copy(q):
        if q < 8:
            ref = f012.at[3 * (q // 4) : 3 * (q // 4) + 3, :, :, (xpos, xdown, xup, xfar)[q % 4], core]
        elif q == 8:
            ref = f3.at[:, :, :, core]
        else:
            ref = f4.at[:, :, :, core]
        return remote(ref, ref, cs.at[q], cr.at[q], other)

    def x_first(c):
        y_done(c)
        x_copy(c, 0).start()
        x_copy(c, 1).start()
        core_copy(4 * c).start()

    def x_forward(c):
        x_copy(c, 0).wait_recv()
        x_copy(c, 2).start()
        core_copy(4 * c + 1).start()
        x_copy(c, 1).wait_recv()
        x_copy(c, 3).start()
        core_copy(4 * c + 2).start()

    def x_done(c):
        x_copy(c, 2).wait_recv()
        x_copy(c, 3).wait_recv()
        core_copy(4 * c + 3).start()

    def core_done(c):
        for q in range(4):
            core_copy(4 * c + q).wait_recv()

    for d in (0, 1, 2, 4, 3):
        home_start(d)
    def block(d, a, part):
        if d <= 2:
            return f012[X_AT[d] + a, part].reshape(W, W)
        if d == 3:
            return f3[a, part].reshape(W, W)
        return f4[a, part].reshape(W, W)

    def d_block(d, part):
        if d <= 2:
            return f012[D_AT[d], part].reshape(W, W)
        return (f3 if d == 3 else f4)[d, part].reshape(W, W)

    def put(high, low, i, real, imag):
        for m, value in enumerate((real, imag, real + imag)):
            high[i, m], low[i, m] = split(value)

    def at(f, e):
        return f * (f - 1) // 2 + e

    def prepare(d):
        def step(e, carry):
            real, imag = block(d, d - 1 - e, 0), block(d, d - 1 - e, 1)
            put(xnh, xnl, at(d, 0) + e, real, imag)
            put(xth, xtl, at(d, 0) + e, real.T, imag.T)
            return carry

        lax.fori_loop(0, d, step, 0)
        put(dnh, dnl, d, d_block(d, 0), d_block(d, 1))

    def three(lefts, rights):
        out = []
        for m in range(3):
            a_high, a_low = lefts(m)
            b_high, b_low = rights(m)
            out.append(mm(a_high, b_high) + mm(a_high, b_low) + mm(a_low, b_high))
        return out[0] - out[1], out[2] - out[0] - out[1]

    def product(high, low, i, bh, bl, j):
        return three(lambda m: (high[i, m], low[i, m]), lambda m: (bh[j, m], bl[j, m]))

    def forward(f, x, xh, xl):
        put(xh, xl, f, x[f, 0], x[f, 1])

        def step(e, carry):
            real, imag = product(xnh, xnl, at(f, e), xh, xl, f)
            x[e, 0] = x[e, 0] - real
            x[e, 1] = x[e, 1] - imag
            return carry

        lax.fori_loop(0, f, step, 0)

    def scale(e, x, xh, xl):
        real, imag = product(dnh, dnl, e, xh, xl, e)
        x[e, 0] = real
        x[e, 1] = imag

    def backward(e, d, x, xh, xl):
        put(xh, xl, e, x[e, 0], x[e, 1])

        def step(f, carry):
            real, imag = product(xth, xtl, at(f, e), xh, xl, e)
            x[f, 0] = x[f, 0] - real
            x[f, 1] = x[f, 1] - imag
            return carry

        lax.fori_loop(e + 1, d, step, 0)

    odd = lax.rem(col, 2) == 1
    second = lax.rem(col, 4) == 2
    whole = lax.rem(col, 8) == 0
    first = jnp.where(odd, 4, jnp.where(second, 3, jnp.where(whole, jnp.where(lax.rem(col, 16) == 0, 1, 2), 0)))
    last = jnp.where(odd, 5, jnp.where(second, 4, jnp.where(whole, 3, 0)))

    def node_out(d, i):
        home = jnp.where(d == 4, col - 1, col - 2)
        src, dst = no.at[lax.rem(d, 2), i], out.at[d * (d + 1) // 2 + i]
        far = remote(src, dst, ns.at[d, i], nr.at[d, i], {"row": row, "col": home})
        near = pltpu.make_async_copy(src, dst, ns.at[d, i])
        return far, near

    def node(d, carry):
        def load(e, c):
            for m in range(2):
                i = at(d, e)
                v[e, m] = xnh[i, m].astype(F32) + xnl[i, m].astype(F32)
            return c

        def forwards(i, c):
            forward(d - 1 - i, v, vh, vl)
            return c

        def scales(e, c):
            scale(e, v, vh, vl)
            return c

        def backwards(e, c):
            backward(e, d, v, vh, vl)
            return c

        lax.fori_loop(0, d, load, 0)
        lax.fori_loop(0, d, forwards, 0)
        lax.fori_loop(0, d, scales, 0)
        lax.fori_loop(0, d, backwards, 0)

        side = lax.rem(d, 2)
        real = (dnh[d, 0, my_rows, :].astype(F32) + dnl[d, 0, my_rows, :].astype(F32))
        imag = (dnh[d, 1, my_rows, :].astype(F32) + dnl[d, 1, my_rows, :].astype(F32))

        def diagonal(e, c):
            i = at(d, e)
            r, m = three(
                lambda m: (xth[i, m, my_rows, :], xtl[i, m, my_rows, :]), lambda m: (vh[e, m], vl[e, m])
            )
            for p in range(2):
                no[side, d - 1 - e, p] = -v[e, p, my_rows, :]
            return c[0] + r, c[1] + m

        real, imag = lax.fori_loop(0, d, diagonal, (real, imag))
        no[side, d, 0] = real
        no[side, d, 1] = imag

        def send(i, c):
            far, near = node_out(d, i)

            @pl.when(d >= 3)
            def _():
                far.start()

            @pl.when(d < 3)
            def _():
                near.start()

            return c

        lax.fori_loop(0, d + 1, send, 0)
        return carry

    def node_finish(d, carry):
        def finish(i, c):
            far, near = node_out(d, i)

            @pl.when(d >= 3)
            def _():
                far.wait_send()

            @pl.when(d < 3)
            def _():
                near.wait()

            return c

        lax.fori_loop(0, d + 1, finish, 0)
        return carry

    def pick(x):
        out = x[:, 0:64]
        for r in range(1, 4):
            out = jnp.where(row == r, x[:, 64 * r : 64 * r + 64], out)
        return out

    def leaf_block(a):
        real, imag = f5[a, 0].reshape(W, W), f5[a, 1].reshape(W, W)
        u[4 - a, 0] = u[4 - a, 0] + real
        u[4 - a, 1] = u[4 - a, 1] + imag
        flipped = jnp.concatenate([pick(real), pick(imag)], axis=1).T
        put(lh, ll, 4 - a, flipped[0:64], flipped[64:128])

    y_first(4)
    piece_wait(0)
    piece_wait(1)
    y_first(0)
    piece_wait(2)
    y_first(1)
    y_first(5)
    y_forward(0)
    y_forward(1)
    piece_wait(4)
    y_first(3)
    x_first(0)
    x_first(1)
    piece_wait(3)
    y_first(2)
    y_first(6)
    y_forward(4)
    y_forward(5)
    x_forward(0)
    y_forward(3)
    x_done(0)
    x_forward(1)
    y_first(7)
    y_first(8)
    y_forward(2)
    d_root.wait()
    root_out = pltpu.make_async_copy(dl.at[1], out.at[0], os.at[0])
    root_out.start()
    u[...] = jnp.zeros_like(u)
    y_done(3)
    core_copy(9).start()
    y_forward(6)
    y_done(4)
    leaf_block(0)
    y_done(5)
    leaf_block(1)
    core_copy(9).wait_recv()
    prepare(4)
    y_done(2)
    core_copy(8).start()
    x_done(1)
    forward(4, u, uh, ul)
    y_forward(7)
    core_copy(8).wait_recv()
    prepare(3)
    core_done(0)
    put(dnh, dnl, 0, d_block(0, 0), d_block(0, 1))
    prepare(1)
    y_forward(8)
    forward(3, u, uh, ul)
    core_done(1)
    prepare(2)
    y_done(6)
    leaf_block(2)
    forward(2, u, uh, ul)
    lax.fori_loop(first, last, node, 0)
    y_done(7)
    leaf_block(3)
    forward(1, u, uh, ul)
    for e in range(1, 5):
        scale(e, u, uh, ul)
    y_done(8)
    leaf_block(4)
    put(uh, ul, 0, u[0, 0], u[0, 1])
    scale(0, u, uh, ul)
    for e in range(5):
        backward(e, 5, u, uh, ul)
    for e in range(5):
        for p in range(2):
            yo[4 - e, p] = -u[e, p, my_rows, :]
    d_leaf.wait()
    copies = [pltpu.make_async_copy(yo.at[0:5], out.at[15:20], os.at[1])]
    copies[0].start()

    def diagonal(e, c):
        r, m = three(lambda m: (lh[e, m], ll[e, m]), lambda m: (uh[e, m], ul[e, m]))
        return c[0] + r, c[1] + m

    yo[5, 0], yo[5, 1] = lax.fori_loop(0, 5, diagonal, (dl[0, 0], dl[0, 1]))
    copies.append(pltpu.make_async_copy(yo.at[5], out.at[20], os.at[2]))
    copies[1].start()

    for d in range(5):
        home_finish(d)
    for n in range(9):
        for q in range(4):
            y_copy(n, q).wait_send()
    for c in range(2):
        for q in range(4):
            x_copy(c, q).wait_send()
    for q in range(10):
        core_copy(q).wait_send()
    lax.fori_loop(first, last, node_finish, 0)
    for d in (3, 4):
        @pl.when(is_home(d))
        def _():
            for i in range(d + 1):
                blk = out.at[d * (d + 1) // 2 + i]
                pltpu.make_async_copy(blk, blk, nr.at[d, i]).wait()
    for copy in [root_out] + copies:
        copy.wait()


def inverse_blocks(st, lp, dg):
    dma = pltpu.SemaphoreType.DMA
    vmem = pltpu.VMEM
    any_spec = pl.BlockSpec(memory_space=pl.ANY)
    return pl.pallas_call(
        kernel,
        out_shape=jax.ShapeDtypeStruct((21, 2, 64, W), F32),
        in_specs=[pl.BlockSpec(memory_space=pltpu.SMEM), any_spec, any_spec],
        out_specs=any_spec,
        scratch_shapes=[
            vmem((6, 2, 4, 4, 2, 8, W), F32),
            vmem((4, 2, 4, 2, 32, W), F32),
            vmem((5, 2, 4, 2, 32, W), F32),
            vmem((5, 2, 4, 64, W), F32),
            vmem((10, 2, 64, W), F32),
            *[vmem((10, 3, W, W), BF16)] * 4,
            *[vmem((5, 3, W, W), BF16)] * 2,
            vmem((5, 2, W, W), F32),
            *[vmem((5, 3, W, W), BF16)] * 2,
            vmem((4, 2, W, W), F32),
            *[vmem((4, 3, W, W), BF16)] * 2,
            *[vmem((5, 3, 64, W), BF16)] * 2,
            vmem((6, 2, 64, W), F32),
            vmem((2, 5, 2, 64, W), F32),
            vmem((2, 2, 64, W), F32),
            dma((5, 2)),
            dma((31, 1)),
            dma((15, 2)),
            dma((7, 2)),
            dma((3, 2)),
            dma((1, 2)),
            dma((9, 4)),
            dma((9, 4)),
            dma((2, 4)),
            dma((2, 4)),
            dma((10,)),
            dma((10,)),
            dma((3,)),
            dma((7,)),
            dma((5, 5)),
            dma((5, 5)),
        ],
        compiler_params=pltpu.CompilerParams(
            vmem_limit_bytes=66_000_000, has_side_effects=True, collective_id=1
        ),
        name="inverse_blocks",
    )(st, lp, dg)


def spread(src, panel, diag, buf, zero, rs, ws):
    col = lax.axis_index("col")

    def active(d):
        return lax.rem(col, 2 ** (5 - d)) == 0

    def read(d):
        at = slice(OUT[d], OUT[d] + d + 1)
        return pltpu.make_async_copy(src.at[at], buf.at[at], rs.at[d])

    for d in range(LEVELS):
        @pl.when(active(d))
        def _():
            read(d).start()

    zero[...] = jnp.zeros_like(zero)
    for d in range(5):
        pltpu.make_async_copy(zero.at[0 : 5 - d], panel.at[d, d:5], ws.at[0, d]).start()

    def write(d, real):
        blocks = buf if real else zero
        at = OUT[d] if real else 0
        out = [pltpu.make_async_copy(blocks.at[at + d if real else 0], diag.at[d], ws.at[1, d])]
        if d:
            out.append(pltpu.make_async_copy(blocks.at[at : at + d], panel.at[d, 0:d], ws.at[2, d]))
        return out

    for d in range(5):
        @pl.when(jnp.logical_not(active(d)))
        def _():
            for copy in write(d, False):
                copy.start()

    for d in range(LEVELS):
        @pl.when(active(d))
        def _():
            read(d).wait()
            for copy in write(d, True):
                copy.start()

    for d in range(5):
        pltpu.make_async_copy(zero.at[0 : 5 - d], panel.at[d, d:5], ws.at[0, d]).wait()
    for d in range(LEVELS):
        for copy in write(d, True):
            copy.wait()


def spread_out(blocks):
    dma = pltpu.SemaphoreType.DMA
    any_spec = pl.BlockSpec(memory_space=pl.ANY)
    return pl.pallas_call(
        spread,
        out_shape=(
            jax.ShapeDtypeStruct((6, 5, 2, 64, W), F32),
            jax.ShapeDtypeStruct((6, 2, 64, W), F32),
        ),
        in_specs=[any_spec],
        out_specs=(any_spec, any_spec),
        scratch_shapes=[
            pltpu.VMEM((21, 2, 64, W), F32),
            pltpu.VMEM((5, 2, 64, W), F32),
            dma((6,)),
            dma((3, 6)),
        ],
        name="spread_out",
    )(blocks)


def body(lower_panel, diag_inverse, structure):
    blocks = inverse_blocks(structure, lower_panel[0], diag_inverse[0])
    panel, diag = spread_out(blocks)
    return panel[None], diag[None]


def solution(mesh):
    in_specs = (
        P("col", None, None, None, "row", None),
        P("col", None, None, "row", None),
        P("col", None, None),
    )
    out_specs = (P("col", None, None, None, "row", None), P("col", None, None, "row", None))
    return jax.shard_map(body, mesh=mesh, in_specs=in_specs, out_specs=out_specs, check_vma=False)
```

```python
import functools

import jax
import jax.numpy as jnp
from jax import lax
from jax.experimental import pallas as pl
from jax.experimental.pallas import tpu as pltpu
from jax.sharding import PartitionSpec as P

LEVELS = 6
MESH = pl.DeviceIdType.MESH
F32 = jnp.float32
BF16 = jnp.bfloat16
W = 256

AT = (None, 0, 1, 3, 6)
OUT = (0, 1, 3, 6, 10, 15)
X_AT = (None, 1, 3)
D_AT = (0, 2, 5)


def split(x):
    high = x.astype(BF16)
    return high, (x - high.astype(F32)).astype(BF16)


def mm(a, b):
    return jnp.dot(a, b, preferred_element_type=F32)


def kernel(
    st, lp, dg, out,
    f012, f3, f4, f5, lv, xnh, xnl, xth, xtl, dnh, dnl, u, uh, ul, v, vh, vl, lh, ll, yo, no, dl,
    p1r, s0, s1, s2, s3, s4, ys, yr, xs, xr, cs, cr, os, ls, ns, nr,
):
    row = lax.axis_index("row")
    col = lax.axis_index("col")
    core = lax.rem(col, 2)
    xpos = lax.rem(col // 2, 4)
    plane = (col // 8) * 8
    up, down = lax.rem(row + 1, 4), lax.rem(row + 3, 4)
    xup, xdown = lax.rem(xpos + 1, 4), lax.rem(xpos + 3, 4)
    xfar = lax.rem(xpos + 2, 4)
    to_row = lambda r: {"row": r, "col": col}
    to_x = lambda x: {"row": row, "col": plane + 2 * x + core}
    other = {"row": row, "col": col + 1 - 2 * core}
    my_rows = pl.ds(pl.multiple_of(row * 64, 64), 64)

    def is_home(d):
        return lax.rem(col, 2 ** (5 - d)) == 0

    def tell(device):
        pl.semaphore_signal(pltpu.get_barrier_semaphore(), inc=1, device_id=device, device_id_type=MESH)

    for device in (other, to_row(up), to_row(down), to_x(xup), to_x(xdown)):
        tell(device)
    for d in range(5):
        @pl.when(jnp.logical_not(is_home(d)))
        def _():
            size = 2 ** (5 - d)
            tell({"row": row, "col": (col // size) * size})

    loads = [pltpu.make_async_copy(lp.at[5], f5.at[:, :, row], ls.at[5])]
    for d in range(1, 5):
        loads.append(pltpu.make_async_copy(lp.at[d, 0:d], lv.at[AT[d] : AT[d] + d], ls.at[d]))
    d_leaf = pltpu.make_async_copy(dg.at[5], dl.at[0], ls.at[0])
    d_root = pltpu.make_async_copy(dg.at[0], dl.at[1], ls.at[6])
    for copy in loads + [d_leaf, d_root]:
        copy.start()
    loads[0].wait()
    for a in range(5):
        f5[a, :, row] = f5[a, :, row] * st[0, 5, a].astype(F32)
    for d in range(1, 5):
        loads[d].wait()
        for a in range(d):
            lv[AT[d] + a] = lv[AT[d] + a] * st[0, d, a].astype(F32)

    callers = 5
    for d in range(5):
        callers = callers + is_home(d).astype(jnp.int32) * (2 ** (5 - d) - 1)
    pl.semaphore_wait(pltpu.get_barrier_semaphore(), callers)

    def remote(src, dst, send, recv, device):
        return pltpu.make_async_remote_copy(
            src_ref=src, dst_ref=dst, send_sem=send, recv_sem=recv, device_id=device, device_id_type=MESH
        )

    def pieces(d, j):
        kk = lax.rem(j, 2)
        mine = lv.at[AT[d] : AT[d] + d] if d else None
        if d <= 2:
            xx = lax.rem(j // 2, 4)
            part = pl.ds(pl.multiple_of(lax.rem(j, 8) * 8, 8), 8)
            out = [(dg.at[d, :, part], f012.at[D_AT[d], :, row, xx, kk])]
            if d:
                out.append((mine.at[:, :, part], f012.at[X_AT[d] : X_AT[d] + d, :, row, xx, kk]))
            return out
        part = pl.ds(pl.multiple_of(kk * 32, 32), 32)
        buf = f3 if d == 3 else f4
        return [
            (dg.at[d, :, part], buf.at[d, :, row, kk]),
            (mine.at[:, :, part], buf.at[0:d, :, row, kk]),
        ]

    sends = (s0, s1, s2, s3, s4)

    def home_copy(d, i, j):
        src, dst = pieces(d, j)[i]
        return remote(src, dst, sends[d].at[j - 1, i], p1r.at[d, i], {"row": row, "col": col + j})

    def n_pieces(d):
        return 2 if d else 1

    def home_start(d):
        @pl.when(is_home(d))
        def _():
            for i, (src, dst) in enumerate(pieces(d, 0)):
                pltpu.make_async_copy(src, dst, p1r.at[d, i]).start()

            def step(j, carry):
                for i in range(n_pieces(d)):
                    home_copy(d, i, j).start()
                return carry

            lax.fori_loop(1, 2 ** (5 - d), step, 0)

    def home_finish(d):
        @pl.when(is_home(d))
        def _():
            def step(j, carry):
                for i in range(n_pieces(d)):
                    home_copy(d, i, j).wait_send()
                return carry

            lax.fori_loop(1, 2 ** (5 - d), step, 0)

    def piece_wait(d):
        for i, (_, dst) in enumerate(pieces(d, lax.rem(col, 8))):
            pltpu.make_async_copy(dst, dst, p1r.at[d, i]).wait()

    def y_slice(n, r, half=None):
        h = slice(None) if half is None else half
        if n < 2:
            return f012.at[3 * n : 3 * n + 3, h, r, xpos, core]
        if n == 2:
            return f3.at[:, h, r, core]
        if n == 3:
            return f4.at[:, h, r, core]
        return f5.at[n - 4, h, r]

    def y_copy(n, q):
        if q == 0:
            ref, device = y_slice(n, row), up
        elif q == 1:
            ref, device = y_slice(n, row), down
        elif q == 2:
            ref, device = y_slice(n, down, 0), up
        else:
            ref, device = y_slice(n, up, 1), down
        return remote(ref, ref, ys.at[n, q], yr.at[n, q], to_row(device))

    def y_first(n):
        y_copy(n, 0).start()
        y_copy(n, 1).start()

    def y_forward(n):
        y_copy(n, 0).wait_recv()
        y_copy(n, 2).start()
        y_copy(n, 1).wait_recv()
        y_copy(n, 3).start()

    def y_done(n):
        y_copy(n, 2).wait_recv()
        y_copy(n, 3).wait_recv()

    def x_copy(c, q):
        blocks = f012.at[3 * c : 3 * c + 3]
        if q == 0:
            ref, device = blocks.at[:, :, :, xpos, core], xup
        elif q == 1:
            ref, device = blocks.at[:, :, :, xpos, core], xdown
        elif q == 2:
            ref, device = blocks.at[:, 0, :, xdown, core], xup
        else:
            ref, device = blocks.at[:, 1, :, xup, core], xdown
        return remote(ref, ref, xs.at[c, q], xr.at[c, q], to_x(device))

    def core_copy(q):
        if q < 8:
            ref = f012.at[3 * (q // 4) : 3 * (q // 4) + 3, :, :, (xpos, xdown, xup, xfar)[q % 4], core]
        elif q == 8:
            ref = f3.at[:, :, :, core]
        else:
            ref = f4.at[:, :, :, core]
        return remote(ref, ref, cs.at[q], cr.at[q], other)

    def x_first(c):
        y_done(c)
        x_copy(c, 0).start()
        x_copy(c, 1).start()
        core_copy(4 * c).start()

    def x_forward(c):
        x_copy(c, 0).wait_recv()
        x_copy(c, 2).start()
        core_copy(4 * c + 1).start()
        x_copy(c, 1).wait_recv()
        x_copy(c, 3).start()
        core_copy(4 * c + 2).start()

    def x_done(c):
        x_copy(c, 2).wait_recv()
        x_copy(c, 3).wait_recv()
        core_copy(4 * c + 3).start()

    def core_done(c):
        for q in range(4):
            core_copy(4 * c + q).wait_recv()

    for d in (0, 1, 2, 4, 3):
        home_start(d)
    def block(d, a, part):
        if d <= 2:
            return f012[X_AT[d] + a, part].reshape(W, W)
        if d == 3:
            return f3[a, part].reshape(W, W)
        return f4[a, part].reshape(W, W)

    def d_block(d, part):
        if d <= 2:
            return f012[D_AT[d], part].reshape(W, W)
        return (f3 if d == 3 else f4)[d, part].reshape(W, W)

    def put(high, low, i, real, imag):
        for m, value in enumerate((real, imag, real + imag)):
            high[i, m], low[i, m] = split(value)

    def at(f, e):
        return f * (f - 1) // 2 + e

    def prepare(d):
        def step(e, carry):
            real, imag = block(d, d - 1 - e, 0), block(d, d - 1 - e, 1)
            put(xnh, xnl, at(d, 0) + e, real, imag)
            put(xth, xtl, at(d, 0) + e, real.T, imag.T)
            return carry

        lax.fori_loop(0, d, step, 0)
        put(dnh, dnl, d, d_block(d, 0), d_block(d, 1))

    def three(lefts, rights):
        out = []
        for m in range(3):
            a_high, a_low = lefts(m)
            b_high, b_low = rights(m)
            out.append(mm(a_high, b_high) + mm(a_high, b_low) + mm(a_low, b_high))
        return out[0] - out[1], out[2] - out[0] - out[1]

    def product(high, low, i, bh, bl, j):
        return three(lambda m: (high[i, m], low[i, m]), lambda m: (bh[j, m], bl[j, m]))

    def forward(f, x, xh, xl):
        put(xh, xl, f, x[f, 0], x[f, 1])

        def step(e, carry):
            real, imag = product(xnh, xnl, at(f, e), xh, xl, f)
            x[e, 0] = x[e, 0] - real
            x[e, 1] = x[e, 1] - imag
            return carry

        lax.fori_loop(0, f, step, 0, unroll=isinstance(f, int))

    def scale(e, x, xh, xl):
        real, imag = product(dnh, dnl, e, xh, xl, e)
        x[e, 0] = real
        x[e, 1] = imag

    def backward(e, d, x, xh, xl):
        put(xh, xl, e, x[e, 0], x[e, 1])

        def step(f, carry):
            real, imag = product(xth, xtl, at(f, e), xh, xl, e)
            x[f, 0] = x[f, 0] - real
            x[f, 1] = x[f, 1] - imag
            return carry

        lax.fori_loop(e + 1, d, step, 0, unroll=isinstance(d, int))

    odd = lax.rem(col, 2) == 1
    second = lax.rem(col, 4) == 2
    whole = lax.rem(col, 8) == 0
    first = jnp.where(odd, 4, jnp.where(second, 3, jnp.where(whole, jnp.where(lax.rem(col, 16) == 0, 1, 2), 0)))
    last = jnp.where(odd, 5, jnp.where(second, 4, jnp.where(whole, 3, 0)))

    def node_copy(d, i):
        src, dst = no.at[d % 2, i], out.at[OUT[d] + i]
        if d >= 3:
            home = {"row": row, "col": col - (1 if d == 4 else 2)}
            return remote(src, dst, ns.at[d, i], nr.at[d, i], home)
        return pltpu.make_async_copy(src, dst, ns.at[d, i])

    def node(d):
        for e in range(d):
            for m in range(2):
                v[e, m] = xnh[at(d, e), m].astype(F32) + xnl[at(d, e), m].astype(F32)
        for f in range(d - 1, -1, -1):
            forward(f, v, vh, vl)
        for e in range(d):
            scale(e, v, vh, vl)
        for e in range(d):
            backward(e, d, v, vh, vl)
        side = d % 2
        real, imag = (dnh[d, m, my_rows, :].astype(F32) + dnl[d, m, my_rows, :].astype(F32) for m in range(2))
        for e in range(d):
            i = at(d, e)
            r, m = three(
                lambda m: (xth[i, m, my_rows, :], xtl[i, m, my_rows, :]), lambda m: (vh[e, m], vl[e, m])
            )
            for p in range(2):
                no[side, d - 1 - e, p] = -v[e, p, my_rows, :]
            real, imag = real + r, imag + m
        no[side, d, 0] = real
        no[side, d, 1] = imag
        for i in range(d + 1):
            node_copy(d, i).start()

    def node_finish(d):
        for i in range(d + 1):
            copy = node_copy(d, i)
            if d >= 3:
                copy.wait_send()
            else:
                copy.wait()

    def nodes(action):
        for d in range(1, 5):
            @pl.when(jnp.logical_and(first <= d, d < last))
            def _():
                action(d)

    def pick(x):
        out = x[:, 0:64]
        for r in range(1, 4):
            out = jnp.where(row == r, x[:, 64 * r : 64 * r + 64], out)
        return out

    def leaf_block(a):
        real, imag = f5[a, 0].reshape(W, W), f5[a, 1].reshape(W, W)
        u[4 - a, 0] = u[4 - a, 0] + real
        u[4 - a, 1] = u[4 - a, 1] + imag
        flipped = jnp.concatenate([pick(real), pick(imag)], axis=1).T
        put(lh, ll, 4 - a, flipped[0:64], flipped[64:128])

    y_first(4)
    y_first(5)
    y_first(6)
    y_forward(4)
    piece_wait(0)
    piece_wait(1)
    y_first(0)
    piece_wait(2)
    y_first(1)
    y_forward(5)
    y_forward(0)
    y_forward(1)
    piece_wait(4)
    y_first(3)
    x_first(0)
    x_first(1)
    piece_wait(3)
    y_first(2)
    y_forward(6)
    d_root.wait()
    root_out = pltpu.make_async_copy(dl.at[1], out.at[0], os.at[0])
    root_out.start()
    u[...] = jnp.zeros_like(u)
    y_done(4)
    leaf_block(0)
    x_forward(0)
    y_done(5)
    leaf_block(1)
    y_forward(3)
    x_done(0)
    y_forward(2)
    x_forward(1)
    y_first(7)
    y_first(8)
    y_done(3)
    core_copy(9).start()
    y_done(6)
    leaf_block(2)
    core_copy(9).wait_recv()
    prepare(4)
    y_done(2)
    core_copy(8).start()
    forward(4, u, uh, ul)
    y_forward(7)
    core_copy(8).wait_recv()
    prepare(3)
    forward(3, u, uh, ul)
    core_done(0)
    put(dnh, dnl, 0, d_block(0, 0), d_block(0, 1))
    prepare(1)
    y_forward(8)
    x_done(1)
    core_done(1)
    prepare(2)
    forward(2, u, uh, ul)
    nodes(node)
    y_done(7)
    leaf_block(3)
    forward(1, u, uh, ul)
    for e in range(1, 5): scale(e, u, uh, ul)
    y_done(8)
    leaf_block(4)
    put(uh, ul, 0, u[0, 0], u[0, 1])
    scale(0, u, uh, ul)
    for e in range(5):
        backward(e, 5, u, uh, ul)
    for e in range(5):
        for p in range(2):
            yo[4 - e, p] = -u[e, p, my_rows, :]
    d_leaf.wait()
    copies = [pltpu.make_async_copy(yo.at[0:5], out.at[15:20], os.at[1])]
    copies[0].start()

    def diagonal(e, c):
        r, m = three(lambda m: (lh[e, m], ll[e, m]), lambda m: (uh[e, m], ul[e, m]))
        return c[0] + r, c[1] + m

    yo[5, 0], yo[5, 1] = lax.fori_loop(0, 5, diagonal, (dl[0, 0], dl[0, 1]))
    copies.append(pltpu.make_async_copy(yo.at[5], out.at[20], os.at[2]))
    copies[1].start()

    for d in range(5):
        home_finish(d)
    for n in range(9):
        for q in range(4):
            y_copy(n, q).wait_send()
    for c in range(2):
        for q in range(4):
            x_copy(c, q).wait_send()
    for q in range(10):
        core_copy(q).wait_send()
    nodes(node_finish)
    for d in (3, 4):
        @pl.when(is_home(d))
        def _():
            for i in range(d + 1):
                blk = out.at[d * (d + 1) // 2 + i]
                pltpu.make_async_copy(blk, blk, nr.at[d, i]).wait()
    for copy in [root_out] + copies:
        copy.wait()


def inverse_blocks(st, lp, dg):
    dma = pltpu.SemaphoreType.DMA
    vmem = pltpu.VMEM
    any_spec = pl.BlockSpec(memory_space=pl.ANY)
    return pl.pallas_call(
        kernel,
        out_shape=jax.ShapeDtypeStruct((21, 2, 64, W), F32),
        in_specs=[pl.BlockSpec(memory_space=pltpu.SMEM), any_spec, any_spec],
        out_specs=any_spec,
        scratch_shapes=[
            vmem((6, 2, 4, 4, 2, 8, W), F32),
            vmem((4, 2, 4, 2, 32, W), F32),
            vmem((5, 2, 4, 2, 32, W), F32),
            vmem((5, 2, 4, 64, W), F32),
            vmem((10, 2, 64, W), F32),
            *[vmem((10, 3, W, W), BF16)] * 4,
            *[vmem((5, 3, W, W), BF16)] * 2,
            vmem((5, 2, W, W), F32),
            *[vmem((5, 3, W, W), BF16)] * 2,
            vmem((4, 2, W, W), F32),
            *[vmem((4, 3, W, W), BF16)] * 2,
            *[vmem((5, 3, 64, W), BF16)] * 2,
            vmem((6, 2, 64, W), F32),
            vmem((2, 5, 2, 64, W), F32),
            vmem((2, 2, 64, W), F32),
            dma((5, 2)),
            dma((31, 1)),
            dma((15, 2)),
            dma((7, 2)),
            dma((3, 2)),
            dma((1, 2)),
            dma((9, 4)),
            dma((9, 4)),
            dma((2, 4)),
            dma((2, 4)),
            dma((10,)),
            dma((10,)),
            dma((3,)),
            dma((7,)),
            dma((5, 5)),
            dma((5, 5)),
        ],
        compiler_params=pltpu.CompilerParams(
            vmem_limit_bytes=66_000_000, has_side_effects=True, collective_id=1
        ),
        name="inverse_blocks",
    )(st, lp, dg)


def spread(src, panel, diag, buf, zero, rs, ws):
    col = lax.axis_index("col")

    def active(d):
        return lax.rem(col, 2 ** (5 - d)) == 0

    def read(d):
        at = slice(OUT[d], OUT[d] + d + 1)
        return pltpu.make_async_copy(src.at[at], buf.at[at], rs.at[d])

    for d in range(LEVELS):
        @pl.when(active(d))
        def _():
            read(d).start()

    zero[...] = jnp.zeros_like(zero)
    for d in range(5):
        pltpu.make_async_copy(zero.at[0 : 5 - d], panel.at[d, d:5], ws.at[0, d]).start()

    def write(d, real):
        blocks = buf if real else zero
        at = OUT[d] if real else 0
        out = [pltpu.make_async_copy(blocks.at[at + d if real else 0], diag.at[d], ws.at[1, d])]
        if d:
            out.append(pltpu.make_async_copy(blocks.at[at : at + d], panel.at[d, 0:d], ws.at[2, d]))
        return out

    for d in range(5):
        @pl.when(jnp.logical_not(active(d)))
        def _():
            for copy in write(d, False):
                copy.start()

    for d in range(LEVELS):
        @pl.when(active(d))
        def _():
            read(d).wait()
            for copy in write(d, True):
                copy.start()

    for d in range(5):
        pltpu.make_async_copy(zero.at[0 : 5 - d], panel.at[d, d:5], ws.at[0, d]).wait()
    for d in range(LEVELS):
        for copy in write(d, True):
            copy.wait()


def spread_out(blocks):
    dma = pltpu.SemaphoreType.DMA
    any_spec = pl.BlockSpec(memory_space=pl.ANY)
    return pl.pallas_call(
        spread,
        out_shape=(
            jax.ShapeDtypeStruct((6, 5, 2, 64, W), F32),
            jax.ShapeDtypeStruct((6, 2, 64, W), F32),
        ),
        in_specs=[any_spec],
        out_specs=(any_spec, any_spec),
        scratch_shapes=[
            pltpu.VMEM((21, 2, 64, W), F32),
            pltpu.VMEM((5, 2, 64, W), F32),
            dma((6,)),
            dma((3, 6)),
        ],
        name="spread_out",
    )(blocks)


def body(lower_panel, diag_inverse, structure):
    blocks = inverse_blocks(structure, lower_panel[0], diag_inverse[0])
    panel, diag = spread_out(blocks)
    return panel[None], diag[None]


def solution(mesh):
    in_specs = (
        P("col", None, None, None, "row", None),
        P("col", None, None, "row", None),
        P("col", None, None),
    )
    out_specs = (P("col", None, None, None, "row", None), P("col", None, None, "row", None))
    return jax.shard_map(body, mesh=mesh, in_specs=in_specs, out_specs=out_specs, check_vma=False)
```

```python
import functools

import jax
import jax.numpy as jnp
from jax import lax
from jax.experimental import pallas as pl
from jax.experimental.pallas import tpu as pltpu
from jax.sharding import PartitionSpec as P

LEVELS = 6
MESH = pl.DeviceIdType.MESH
F32 = jnp.float32
BF16 = jnp.bfloat16
W = 256

AT = (None, 0, 1, 3, 6)
OUT = (0, 1, 3, 6, 10, 15)
X_AT = (None, 1, 3)
D_AT = (0, 2, 5)


def split(x):
    high = x.astype(BF16)
    return high, (x - high.astype(F32)).astype(BF16)


def mm(a, b):
    return jnp.dot(a, b, preferred_element_type=F32)


def kernel(
    st, lp, dg, out,
    f012, f3, f4, f5, lv, xnh, xnl, xth, xtl, dnh, dnl, u, uh, ul, v, vh, vl, lh, ll, yo, no, dl, sv,
    p1r, s0, s1, s2, s3, s4, ys, yr, xs, xr, cs, cr, os, ls, ns, nr,
):
    row = lax.axis_index("row")
    col = lax.axis_index("col")
    core = lax.rem(col, 2)
    xpos = lax.rem(col // 2, 4)
    plane = (col // 8) * 8
    up, down = lax.rem(row + 1, 4), lax.rem(row + 3, 4)
    xup, xdown = lax.rem(xpos + 1, 4), lax.rem(xpos + 3, 4)
    xfar = lax.rem(xpos + 2, 4)
    to_row = lambda r: {"row": r, "col": col}
    to_x = lambda x: {"row": row, "col": plane + 2 * x + core}
    other = {"row": row, "col": col + 1 - 2 * core}
    my_rows = pl.ds(pl.multiple_of(row * 64, 64), 64)

    def is_home(d):
        return lax.rem(col, 2 ** (5 - d)) == 0

    def tell(device):
        pl.semaphore_signal(pltpu.get_barrier_semaphore(), inc=1, device_id=device, device_id_type=MESH)

    for device in (other, to_row(up), to_row(down), to_x(xup), to_x(xdown)):
        tell(device)
    for d in range(5):
        @pl.when(jnp.logical_not(is_home(d)))
        def _():
            size = 2 ** (5 - d)
            tell({"row": row, "col": (col // size) * size})

    loads = [pltpu.make_async_copy(lp.at[5], f5.at[:, :, row], ls.at[5])]
    for d in range(1, 5):
        loads.append(pltpu.make_async_copy(lp.at[d, 0:d], lv.at[AT[d] : AT[d] + d], ls.at[d]))
    d_leaf = pltpu.make_async_copy(dg.at[5], dl.at[0], ls.at[0])
    d_root = pltpu.make_async_copy(dg.at[0], dl.at[1], ls.at[6])
    flags = pltpu.make_async_copy(st, sv, ls.at[7])
    for copy in [flags] + loads + [d_leaf, d_root]:
        copy.start()
    flags.wait()

    def flag(d, a):
        return sv[0, d : d + 1, a : a + 1].astype(F32)

    loads[0].wait()
    for a in range(5):
        f5[a, :, row] = f5[a, :, row] * flag(5, a)
    for d in range(1, 5):
        loads[d].wait()
        for a in range(d):
            lv[AT[d] + a] = lv[AT[d] + a] * flag(d, a)

    callers = 5
    for d in range(5):
        callers = callers + is_home(d).astype(jnp.int32) * (2 ** (5 - d) - 1)
    pl.semaphore_wait(pltpu.get_barrier_semaphore(), callers)

    def remote(src, dst, send, recv, device):
        return pltpu.make_async_remote_copy(
            src_ref=src, dst_ref=dst, send_sem=send, recv_sem=recv, device_id=device, device_id_type=MESH
        )

    def pieces(d, j):
        kk = lax.rem(j, 2)
        mine = lv.at[AT[d] : AT[d] + d] if d else None
        if d <= 2:
            xx = lax.rem(j // 2, 4)
            part = pl.ds(pl.multiple_of(lax.rem(j, 8) * 8, 8), 8)
            out = [(dg.at[d, :, part], f012.at[D_AT[d], :, row, xx, kk])]
            if d:
                out.append((mine.at[:, :, part], f012.at[X_AT[d] : X_AT[d] + d, :, row, xx, kk]))
            return out
        part = pl.ds(pl.multiple_of(kk * 32, 32), 32)
        buf = f3 if d == 3 else f4
        return [
            (dg.at[d, :, part], buf.at[d, :, row, kk]),
            (mine.at[:, :, part], buf.at[0:d, :, row, kk]),
        ]

    sends = (s0, s1, s2, s3, s4)

    def home_copy(d, i, j):
        src, dst = pieces(d, j)[i]
        return remote(src, dst, sends[d].at[j - 1, i], p1r.at[d, i], {"row": row, "col": col + j})

    def n_pieces(d):
        return 2 if d else 1

    def home_start(d):
        @pl.when(is_home(d))
        def _():
            for i, (src, dst) in enumerate(pieces(d, 0)):
                pltpu.make_async_copy(src, dst, p1r.at[d, i]).start()

            def step(j, carry):
                for i in range(n_pieces(d)):
                    home_copy(d, i, j).start()
                return carry

            lax.fori_loop(1, 2 ** (5 - d), step, 0)

    def home_finish(d):
        @pl.when(is_home(d))
        def _():
            def step(j, carry):
                for i in range(n_pieces(d)):
                    home_copy(d, i, j).wait_send()
                return carry

            lax.fori_loop(1, 2 ** (5 - d), step, 0)

    def piece_wait(d):
        for i, (_, dst) in enumerate(pieces(d, lax.rem(col, 8))):
            pltpu.make_async_copy(dst, dst, p1r.at[d, i]).wait()

    def y_slice(n, r, half=None):
        h = slice(None) if half is None else half
        if n < 2:
            return f012.at[3 * n : 3 * n + 3, h, r, xpos, core]
        if n == 2:
            return f3.at[:, h, r, core]
        if n == 3:
            return f4.at[:, h, r, core]
        return f5.at[n - 4, h, r]

    def y_copy(n, q):
        if q == 0:
            ref, device = y_slice(n, row), up
        elif q == 1:
            ref, device = y_slice(n, row), down
        elif q == 2:
            ref, device = y_slice(n, down, 0), up
        else:
            ref, device = y_slice(n, up, 1), down
        return remote(ref, ref, ys.at[n, q], yr.at[n, q], to_row(device))

    def y_first(n):
        y_copy(n, 0).start()
        y_copy(n, 1).start()

    def y_forward(n):
        y_copy(n, 0).wait_recv()
        y_copy(n, 2).start()
        y_copy(n, 1).wait_recv()
        y_copy(n, 3).start()

    def y_done(n):
        y_copy(n, 2).wait_recv()
        y_copy(n, 3).wait_recv()

    def x_copy(c, q):
        blocks = f012.at[3 * c : 3 * c + 3]
        if q == 0:
            ref, device = blocks.at[:, :, :, xpos, core], xup
        elif q == 1:
            ref, device = blocks.at[:, :, :, xpos, core], xdown
        elif q == 2:
            ref, device = blocks.at[:, 0, :, xdown, core], xup
        else:
            ref, device = blocks.at[:, 1, :, xup, core], xdown
        return remote(ref, ref, xs.at[c, q], xr.at[c, q], to_x(device))

    def core_copy(q):
        if q < 8:
            ref = f012.at[3 * (q // 4) : 3 * (q // 4) + 3, :, :, (xpos, xdown, xup, xfar)[q % 4], core]
        elif q == 8:
            ref = f3.at[:, :, :, core]
        else:
            ref = f4.at[:, :, :, core]
        return remote(ref, ref, cs.at[q], cr.at[q], other)

    def x_first(c):
        y_done(c)
        x_copy(c, 0).start()
        x_copy(c, 1).start()
        core_copy(4 * c).start()

    def x_forward(c):
        x_copy(c, 0).wait_recv()
        x_copy(c, 2).start()
        core_copy(4 * c + 1).start()
        x_copy(c, 1).wait_recv()
        x_copy(c, 3).start()
        core_copy(4 * c + 2).start()

    def x_done(c):
        x_copy(c, 2).wait_recv()
        x_copy(c, 3).wait_recv()
        core_copy(4 * c + 3).start()

    def core_done(c):
        for q in range(4):
            core_copy(4 * c + q).wait_recv()

    for d in (0, 1, 2, 4, 3):
        home_start(d)
    def block(d, a, part):
        if d <= 2:
            return f012[X_AT[d] + a, part].reshape(W, W)
        if d == 3:
            return f3[a, part].reshape(W, W)
        return f4[a, part].reshape(W, W)

    def d_block(d, part):
        if d <= 2:
            return f012[D_AT[d], part].reshape(W, W)
        return (f3 if d == 3 else f4)[d, part].reshape(W, W)

    def put(high, low, i, real, imag):
        for m, value in enumerate((real, imag, real + imag)):
            high[i, m], low[i, m] = split(value)

    def at(f, e):
        return f * (f - 1) // 2 + e

    def prepare(d):
        def step(e, carry):
            real, imag = block(d, d - 1 - e, 0), block(d, d - 1 - e, 1)
            put(xnh, xnl, at(d, 0) + e, real, imag)
            put(xth, xtl, at(d, 0) + e, real.T, imag.T)
            return carry

        lax.fori_loop(0, d, step, 0)
        put(dnh, dnl, d, d_block(d, 0), d_block(d, 1))

    def three(lefts, rights):
        out = []
        for m in range(3):
            a_high, a_low = lefts(m)
            b_high, b_low = rights(m)
            out.append(mm(a_high, b_high) + mm(a_high, b_low) + mm(a_low, b_high))
        return out[0] - out[1], out[2] - out[0] - out[1]

    def product(high, low, i, bh, bl, j):
        return three(lambda m: (high[i, m], low[i, m]), lambda m: (bh[j, m], bl[j, m]))

    def forward(f, x, xh, xl):
        put(xh, xl, f, x[f, 0], x[f, 1])

        def step(e, carry):
            real, imag = product(xnh, xnl, at(f, e), xh, xl, f)
            x[e, 0] = x[e, 0] - real
            x[e, 1] = x[e, 1] - imag
            return carry

        lax.fori_loop(0, f, step, 0, unroll=isinstance(f, int))

    def scale(e, x, xh, xl):
        real, imag = product(dnh, dnl, e, xh, xl, e)
        x[e, 0] = real
        x[e, 1] = imag

    def backward(e, d, x, xh, xl):
        put(xh, xl, e, x[e, 0], x[e, 1])

        def step(f, carry):
            real, imag = product(xth, xtl, at(f, e), xh, xl, e)
            x[f, 0] = x[f, 0] - real
            x[f, 1] = x[f, 1] - imag
            return carry

        lax.fori_loop(e + 1, d, step, 0, unroll=isinstance(d, int))

    odd = lax.rem(col, 2) == 1
    second = lax.rem(col, 4) == 2
    whole = lax.rem(col, 8) == 0
    first = jnp.where(odd, 4, jnp.where(second, 3, jnp.where(whole, jnp.where(lax.rem(col, 16) == 0, 1, 2), 0)))
    last = jnp.where(odd, 5, jnp.where(second, 4, jnp.where(whole, 3, 0)))

    def node_copy(d, i):
        src, dst = no.at[d % 2, i], out.at[OUT[d] + i]
        if d >= 3:
            home = {"row": row, "col": col - (1 if d == 4 else 2)}
            return remote(src, dst, ns.at[d, i], nr.at[d, i], home)
        return pltpu.make_async_copy(src, dst, ns.at[d, i])

    def node(d):
        for e in range(d):
            for m in range(2):
                v[e, m] = xnh[at(d, e), m].astype(F32) + xnl[at(d, e), m].astype(F32)
        for f in range(d - 1, -1, -1):
            forward(f, v, vh, vl)
        for e in range(d):
            scale(e, v, vh, vl)
        for e in range(d):
            backward(e, d, v, vh, vl)
        side = d % 2
        real, imag = (dnh[d, m, my_rows, :].astype(F32) + dnl[d, m, my_rows, :].astype(F32) for m in range(2))
        for e in range(d):
            i = at(d, e)
            r, m = three(
                lambda m: (xth[i, m, my_rows, :], xtl[i, m, my_rows, :]), lambda m: (vh[e, m], vl[e, m])
            )
            for p in range(2):
                no[side, d - 1 - e, p] = -v[e, p, my_rows, :]
            real, imag = real + r, imag + m
        no[side, d, 0] = real
        no[side, d, 1] = imag
        for i in range(d + 1):
            node_copy(d, i).start()

    def node_finish(d):
        for i in range(d + 1):
            copy = node_copy(d, i)
            if d >= 3:
                copy.wait_send()
            else:
                copy.wait()

    def nodes(action):
        for d in range(1, 5):
            @pl.when(jnp.logical_and(first <= d, d < last))
            def _():
                action(d)

    def pick(x):
        out = x[:, 0:64]
        for r in range(1, 4):
            out = jnp.where(row == r, x[:, 64 * r : 64 * r + 64], out)
        return out

    def leaf_block(a):
        real, imag = f5[a, 0].reshape(W, W), f5[a, 1].reshape(W, W)
        u[4 - a, 0] = u[4 - a, 0] + real
        u[4 - a, 1] = u[4 - a, 1] + imag
        flipped = jnp.concatenate([pick(real), pick(imag)], axis=1).T
        put(lh, ll, 4 - a, flipped[0:64], flipped[64:128])

    y_first(4)
    y_first(5)
    y_first(6)
    y_forward(4)
    piece_wait(0)
    piece_wait(1)
    y_first(0)
    piece_wait(2)
    y_first(1)
    y_forward(5)
    y_forward(0)
    y_forward(1)
    piece_wait(4)
    y_first(3)
    x_first(0)
    x_first(1)
    piece_wait(3)
    y_first(2)
    y_forward(6)
    d_root.wait()
    root_out = pltpu.make_async_copy(dl.at[1], out.at[0], os.at[0])
    root_out.start()
    u[...] = jnp.zeros_like(u)
    y_done(4)
    leaf_block(0)
    x_forward(0)
    y_done(5)
    leaf_block(1)
    y_forward(3)
    x_done(0)
    y_forward(2)
    x_forward(1)
    y_first(7)
    y_first(8)
    y_done(3)
    core_copy(9).start()
    y_done(6)
    leaf_block(2)
    core_copy(9).wait_recv()
    prepare(4)
    y_done(2)
    core_copy(8).start()
    forward(4, u, uh, ul)
    y_forward(7)
    core_copy(8).wait_recv()
    prepare(3)
    forward(3, u, uh, ul)
    core_done(0)
    put(dnh, dnl, 0, d_block(0, 0), d_block(0, 1))
    prepare(1)
    y_forward(8)
    x_done(1)
    core_done(1)
    prepare(2)
    forward(2, u, uh, ul)
    nodes(node)
    y_done(7)
    leaf_block(3)
    forward(1, u, uh, ul)
    for e in range(1, 5): scale(e, u, uh, ul)
    y_done(8)
    leaf_block(4)
    put(uh, ul, 0, u[0, 0], u[0, 1])
    scale(0, u, uh, ul)
    for e in range(5):
        backward(e, 5, u, uh, ul)
    for e in range(5):
        for p in range(2):
            yo[4 - e, p] = -u[e, p, my_rows, :]
    d_leaf.wait()
    copies = [pltpu.make_async_copy(yo.at[0:5], out.at[15:20], os.at[1])]
    copies[0].start()

    def diagonal(e, c):
        r, m = three(lambda m: (lh[e, m], ll[e, m]), lambda m: (uh[e, m], ul[e, m]))
        return c[0] + r, c[1] + m

    yo[5, 0], yo[5, 1] = lax.fori_loop(0, 5, diagonal, (dl[0, 0], dl[0, 1]))
    copies.append(pltpu.make_async_copy(yo.at[5], out.at[20], os.at[2]))
    copies[1].start()

    for d in range(5):
        home_finish(d)
    for n in range(9):
        for q in range(4):
            y_copy(n, q).wait_send()
    for c in range(2):
        for q in range(4):
            x_copy(c, q).wait_send()
    for q in range(10):
        core_copy(q).wait_send()
    nodes(node_finish)
    for d in (3, 4):
        @pl.when(is_home(d))
        def _():
            for i in range(d + 1):
                blk = out.at[d * (d + 1) // 2 + i]
                pltpu.make_async_copy(blk, blk, nr.at[d, i]).wait()
    for copy in [root_out] + copies:
        copy.wait()


def inverse_blocks(st, lp, dg):
    dma = pltpu.SemaphoreType.DMA
    vmem = pltpu.VMEM
    any_spec = pl.BlockSpec(memory_space=pl.ANY)
    return pl.pallas_call(
        kernel,
        out_shape=jax.ShapeDtypeStruct((21, 2, 64, W), F32),
        in_specs=[any_spec, any_spec, any_spec],
        out_specs=any_spec,
        scratch_shapes=[
            vmem((6, 2, 4, 4, 2, 8, W), F32),
            vmem((4, 2, 4, 2, 32, W), F32),
            vmem((5, 2, 4, 2, 32, W), F32),
            vmem((5, 2, 4, 64, W), F32),
            vmem((10, 2, 64, W), F32),
            *[vmem((10, 3, W, W), BF16)] * 4,
            *[vmem((5, 3, W, W), BF16)] * 2,
            vmem((5, 2, W, W), F32),
            *[vmem((5, 3, W, W), BF16)] * 2,
            vmem((4, 2, W, W), F32),
            *[vmem((4, 3, W, W), BF16)] * 2,
            *[vmem((5, 3, 64, W), BF16)] * 2,
            vmem((6, 2, 64, W), F32),
            vmem((2, 5, 2, 64, W), F32),
            vmem((2, 2, 64, W), F32),
            vmem((1, 6, 5), jnp.int32),
            dma((5, 2)),
            dma((31, 1)),
            dma((15, 2)),
            dma((7, 2)),
            dma((3, 2)),
            dma((1, 2)),
            dma((9, 4)),
            dma((9, 4)),
            dma((2, 4)),
            dma((2, 4)),
            dma((10,)),
            dma((10,)),
            dma((3,)),
            dma((8,)),
            dma((5, 5)),
            dma((5, 5)),
        ],
        compiler_params=pltpu.CompilerParams(
            vmem_limit_bytes=66_000_000, has_side_effects=True, collective_id=1
        ),
        name="inverse_blocks",
    )(st, lp, dg)


def spread(src, panel, diag, buf, zero, rs, ws):
    col = lax.axis_index("col")

    def active(d):
        return lax.rem(col, 2 ** (5 - d)) == 0

    def read(d):
        at = slice(OUT[d], OUT[d] + d + 1)
        return pltpu.make_async_copy(src.at[at], buf.at[at], rs.at[d])

    for d in range(LEVELS):
        @pl.when(active(d))
        def _():
            read(d).start()

    zero[...] = jnp.zeros_like(zero)
    for d in range(5):
        pltpu.make_async_copy(zero.at[0 : 5 - d], panel.at[d, d:5], ws.at[0, d]).start()

    def write(d, real):
        blocks = buf if real else zero
        at = OUT[d] if real else 0
        out = [pltpu.make_async_copy(blocks.at[at + d if real else 0], diag.at[d], ws.at[1, d])]
        if d:
            out.append(pltpu.make_async_copy(blocks.at[at : at + d], panel.at[d, 0:d], ws.at[2, d]))
        return out

    for d in range(5):
        @pl.when(jnp.logical_not(active(d)))
        def _():
            for copy in write(d, False):
                copy.start()

    for d in range(LEVELS):
        @pl.when(active(d))
        def _():
            read(d).wait()
            for copy in write(d, True):
                copy.start()

    for d in range(5):
        pltpu.make_async_copy(zero.at[0 : 5 - d], panel.at[d, d:5], ws.at[0, d]).wait()
    for d in range(LEVELS):
        for copy in write(d, True):
            copy.wait()


def spread_out(blocks):
    dma = pltpu.SemaphoreType.DMA
    any_spec = pl.BlockSpec(memory_space=pl.ANY)
    return pl.pallas_call(
        spread,
        out_shape=(
            jax.ShapeDtypeStruct((6, 5, 2, 64, W), F32),
            jax.ShapeDtypeStruct((6, 2, 64, W), F32),
        ),
        in_specs=[any_spec],
        out_specs=(any_spec, any_spec),
        scratch_shapes=[
            pltpu.VMEM((21, 2, 64, W), F32),
            pltpu.VMEM((5, 2, 64, W), F32),
            dma((6,)),
            dma((3, 6)),
        ],
        name="spread_out",
    )(blocks)


def body(lower_panel, diag_inverse, structure):
    blocks = inverse_blocks(structure, lower_panel[0], diag_inverse[0])
    panel, diag = spread_out(blocks)
    return panel[None], diag[None]


def solution(mesh):
    in_specs = (
        P("col", None, None, None, "row", None),
        P("col", None, None, "row", None),
        P("col", None, None),
    )
    out_specs = (P("col", None, None, None, "row", None), P("col", None, None, "row", None))
    return jax.shard_map(body, mesh=mesh, in_specs=in_specs, out_specs=out_specs, check_vma=False)
```
